32 devices in a mesh: dp: 8 (over y, x, core), mp: 4 (over z).
Axes of the slice: x: 2, y: 2, z: 4, core: 2. Of those that a mesh axis runs over, the one named last changes fastest.
Arguments:
- gen_rows: bfloat16 [1024, 5120], P(('dp', 'mp')), may hold values from -6 to 6
- lengths: int32 [32, 4], P('dp'), may hold values from 1 to 16, 32 in all within a row
- assign: int32 [32, 4], P('dp'), may hold values from 0 to 3, each once within a row
- rewards: float32 [32, 4], P('dp'), may hold values from 0 to 1
- upstream: bfloat16 [2048, 2048], P('dp', 'mp'), may hold values from -6 to 6
- weight: bfloat16 [5120, 2048], P(None, 'mp'), may hold values from -0.078125 to 0.078125
- q_init: float32 [2048, 64], P('mp'), may hold values from -6 to 6
- resid: float32 [32, 128, 2048], P('dp', None, 'mp'), may hold values from -4 to 4
- block_ids: int32 [32], P('dp'), may hold values from 0 to 39, as said below
Outputs:
- p_factor: float32 [5120, 256], P(None, 'mp')
- q_factor: float32 [2048, 64], P('mp')
- resid_out: float32 [32, 128, 2048], P('dp', None, 'mp')
The draws below stay inside these ranges and needn't reach their ends.
Inputs may be any that keep to these rules, and one draw needn't show every extreme that they name: Each row holds the lengths of one generator's 4 sequences; they sum to 32. `assign`: each row names every learner once. `block_ids`: the 4 ids of one replica are distinct.
All inputs are finite; a program needn't handle non-finite values.
Results may differ from the reference program's by a relative error of at most 0.003.
Values may be sent and summed in bfloat16 or wider, within the bound.
No kernel may reach another device: no remote copies, remote signals or barrier semaphores. Data moves between devices by JAX's collectives and lax.ppermute only.
A program may use at most 64 MiB of HBM per device.

```python
import math
import jax
import jax.numpy as jnp
import numpy as np
from jax import lax

D = 5120
KVW = 2048
RANK = 64
CAP = 16
BLK = 128
KBLK = 4
SEQS = 4
SLOTS = 32
N_DP = 8
N_MP = 4


def draw_block_ids(key, part):
    keys = jax.random.split(jax.random.fold_in(key, 17), N_DP)

    def one_replica(replica_key):
        return jax.random.permutation(replica_key, D // BLK)[:KBLK].astype(jnp.int32)
    return jax.vmap(one_replica)(keys).reshape(N_DP * KBLK)


def level_of(own_key, extent, pieces, least, top_value):
    loudness, own = 1.0, jax.random.fold_in(own_key, 6)
    for axis_at, parts in pieces:
        draws = jnp.exp(jax.random.uniform(jax.random.fold_in(own, axis_at), (parts,), jnp.float32, least / len(pieces), top_value / len(pieces)))
        loudness = loudness * jnp.repeat(draws, extent[axis_at] // parts).reshape([-1 if axis == axis_at else 1 for axis in range(len(extent))])
    return loudness


def length_profile(amount, total, reach, skew):
    loads = [(1 << 20) // math.isqrt(grade ** skew) + 1 for grade in range(2, amount + 1)]
    spare, counts = total - reach - (amount - 1), [1] * (amount - 1)
    while spare > 0:
        candidates = [i for i in range(amount - 1) if counts[i] < reach]
        mass, remaining = sum([loads[i] for i in candidates]), spare
        for i in candidates:
            addition = min(reach - counts[i], max(1, remaining * loads[i] // mass), spare)
            counts[i] = counts[i] + addition
            spare = spare - addition
    return np.array([reach] + counts)


def ragged(rng, number_of, total, limit, lean):
    if number_of == 2:
        one = jax.random.randint(rng, (), max(1, total - limit), min(limit, total - 1) + 1)
        return jnp.stack([one, total - one])
    tallies = jnp.asarray(length_profile(number_of, total, limit, lean), jnp.int32)
    couples = (number_of - 1) // 2
    source_of, receiver = tallies[1:1 + 2 * couples:2], tallies[2:2 + 2 * couples:2]
    margin = jnp.minimum(source_of - 1, limit - receiver)
    shifted = jax.random.randint(jax.random.fold_in(rng, 1), (couples,), 0, 1 << 20) % (margin + 1)
    tallies = tallies.at[1:1 + 2 * couples:2].set(source_of - shifted).at[2:2 + 2 * couples:2].set(receiver + shifted)
    return tallies[jax.random.permutation(jax.random.fold_in(rng, 2), number_of)]


def scatter_about(own_key, dims, width, most, pieces=(), held_as=jnp.bfloat16):
    array = width * jax.random.normal(own_key, dims, jnp.float32)
    if pieces:
        array = array * level_of(own_key, dims, pieces, -0.22, 0.18)
    return jnp.clip(array, -most, most).astype(held_as)


def setup_inputs(seed: int = 0) -> dict:
    streams_of = jax.random.split(jax.random.key(seed), 10)
    gen_rows = scatter_about(streams_of[0], (N_DP * N_MP * SLOTS, D), 1.0, 6.0, ((0, 32),))
    lengths = jax.vmap(lambda own: ragged(own, SEQS, SLOTS, CAP, 2))(jax.random.split(streams_of[1], (N_DP * N_MP))).reshape((N_DP * N_MP, SEQS)).astype(jnp.int32)
    assign = jax.vmap(lambda own: jax.random.permutation(own, N_MP))(jax.random.split(streams_of[2], (N_DP * N_MP))).reshape((N_DP * N_MP, N_MP)).astype(jnp.int32)
    rewards = jnp.clip(1.0 * jax.random.uniform(streams_of[3], (N_DP * N_MP, SEQS), jnp.float32) ** level_of(streams_of[3], (N_DP * N_MP, SEQS), ((0, 8),), -0.2, 0.2), 0.0, 1.0)
    upstream = scatter_about(streams_of[4], (N_DP * N_MP * N_MP * CAP, KVW), 1.0, 6.0, ((0, 8), (1, 4)))
    weight = scatter_about(streams_of[5], (D, KVW), D ** -0.5, 0.078125, ((1, 4),))
    q_init = scatter_about(streams_of[6], (KVW, RANK), 1.0, 6.0, ((0, 4),), jnp.float32)
    resid = scatter_about(streams_of[7], (N_DP * KBLK, BLK, KVW), 0.5, 4.0, ((0, 8), (2, 4)), jnp.float32)
    block_ids = draw_block_ids(jax.random.fold_in(streams_of[9], 71), 0)
    return dict(gen_rows=gen_rows, lengths=lengths, assign=assign, rewards=rewards, upstream=upstream, weight=weight, q_init=q_init, resid=resid, block_ids=block_ids)


HIGHEST_PRECISION = lax.Precision.HIGHEST

def packed_tables(lengths, assign, rewards, slot_count, capacity):
    groups, sequences = lengths.shape
    offsets = (jnp.cumsum(lengths, axis=1) - lengths).astype(jnp.int32)
    advantage = rewards - lax.optimization_barrier(jnp.mean(rewards, axis=1, keepdims=True))
    seq_weight = advantage / lengths.astype(rewards.dtype)
    positions = jnp.arange(slot_count).astype(jnp.int32)
    seq_index = jnp.arange(sequences).astype(jnp.int32)
    inside = (offsets[:, None, :] <= positions[None, :, None]).astype(jnp.int32)
    owner = (lax.optimization_barrier(jnp.sum(inside, axis=2)) - 1).astype(jnp.int32)
    picked = owner[:, :, None] == seq_index[None, None, :]
    seq_start = lax.optimization_barrier(jnp.sum(jnp.where(picked, offsets[:, None, :], 0), axis=2)).astype(jnp.int32)
    learner = lax.optimization_barrier(jnp.sum(jnp.where(picked, assign[:, None, :], 0), axis=2)).astype(jnp.int32)
    row_weight = lax.optimization_barrier(jnp.sum(jnp.where(picked, seq_weight[:, None, :], 0.0), axis=2))
    source = jnp.arange(groups).astype(jnp.int32)[:, None]
    slot_table = learner * (groups * capacity) + source * capacity + positions[None, :] - seq_start
    return (slot_table.astype(jnp.int32), row_weight)

def hidden_grad(row_block, upstream_rows, row_weight, weight):
    hidden = jnp.dot(row_block.astype(jnp.float32), weight.astype(jnp.float32), preferred_element_type=jnp.float32)
    tangent = jnp.tanh(hidden)
    return (row_weight[:, None] * upstream_rows.astype(jnp.float32) * (1.0 - tangent * tangent)).astype(jnp.bfloat16)

def orthonormal(p_part):
    gram_matrix = jnp.dot(p_part.T, p_part, precision=HIGHEST_PRECISION)
    factor_low = jnp.linalg.cholesky(gram_matrix)
    return jax.scipy.linalg.solve_triangular(factor_low, p_part.T, lower=True).T

def reference(gen_rows, lengths, assign, rewards, upstream, weight, q_init, resid, block_ids):
    shard_cols = KVW // N_MP
    group_rows = gen_rows.reshape(N_DP, N_MP * SLOTS, D)
    group_lengths = lengths.reshape(N_DP, N_MP, SEQS)
    group_assign = assign.reshape(N_DP, N_MP, N_MP)
    group_rewards = rewards.reshape(N_DP, N_MP, SEQS)
    group_upstream = upstream.reshape(N_DP, N_MP * N_MP * CAP, KVW)
    group_resid = resid.reshape(N_DP, KBLK, BLK, KVW)
    group_ids = block_ids.reshape(N_DP, KBLK)
    q_parts = q_init.reshape(N_MP, shard_cols, RANK)

    def first_pass(p_total, inputs):
        row_block, lengths_here, assign_here, rewards_here, upstream_here, resid_here, ids_here = inputs
        slot_table, row_weight = packed_tables(lengths_here, assign_here, rewards_here, SLOTS, CAP)
        upstream_rows = jnp.take(upstream_here, slot_table.reshape(-1), axis=0)
        grad_h = hidden_grad(row_block, upstream_rows, row_weight.reshape(-1), weight)
        wide_rows = row_block.astype(jnp.float32)
        projected = jnp.einsum('nmc,mcr->nmr', grad_h.astype(jnp.float32).reshape(-1, N_MP, shard_cols), q_parts, precision=HIGHEST_PRECISION)
        p_term = jnp.einsum('nd,nk->dk', wide_rows, projected.reshape(-1, N_MP * RANK), precision=HIGHEST_PRECISION)
        resid_proj = jnp.einsum('kbmc,mcr->kbmr', resid_here.reshape(KBLK, BLK, N_MP, shard_cols), q_parts, precision=HIGHEST_PRECISION).reshape(KBLK, BLK, N_MP * RANK)
        for block in range(KBLK):
            first_row = (ids_here[block] * BLK).astype(jnp.int32)
            current = lax.dynamic_slice_in_dim(p_term, first_row, BLK, 0)
            p_term = lax.dynamic_update_slice_in_dim(p_term, current + resid_proj[block], first_row, 0)
        return (p_total + p_term, grad_h)
    p_start = jnp.zeros((D, N_MP * RANK), jnp.float32)
    p_sum, grad_all = lax.scan(first_pass, p_start, (group_rows, group_lengths, group_assign, group_rewards, group_upstream, group_resid, group_ids))
    p_parts = jnp.transpose(p_sum.reshape(D, N_MP, RANK), (1, 0, 2))
    p_hat = jax.vmap(orthonormal)(p_parts)
    p_flat = jnp.transpose(p_hat, (1, 0, 2)).reshape(D, N_MP * RANK)

    def second_pass(q_total, inputs):
        row_block, grad_h, resid_here, ids_here = inputs
        wide_rows = row_block.astype(jnp.float32)
        wide_grad = grad_h.astype(jnp.float32)
        row_proj = jnp.dot(wide_rows, p_flat, precision=HIGHEST_PRECISION)
        q_term = jnp.einsum('nmc,nmr->mcr', wide_grad.reshape(-1, N_MP, shard_cols), row_proj.reshape(-1, N_MP, RANK), precision=HIGHEST_PRECISION)
        merged_blocks = []
        for block in range(KBLK):
            first_row = (ids_here[block] * BLK).astype(jnp.int32)
            columns = lax.dynamic_slice_in_dim(wide_rows, first_row, BLK, 1)
            grad_block = jnp.einsum('nb,nk->bk', columns, wide_grad, precision=HIGHEST_PRECISION)
            p_rows = lax.dynamic_slice_in_dim(p_flat, first_row, BLK, 0)
            q_term = q_term + jnp.einsum('bmc,bmr->mcr', resid_here[block].reshape(BLK, N_MP, shard_cols), p_rows.reshape(BLK, N_MP, RANK), precision=HIGHEST_PRECISION)
            merged_blocks.append(grad_block + resid_here[block])
        return (q_total + q_term, jnp.stack(merged_blocks))
    q_start = jnp.zeros((N_MP, shard_cols, RANK), jnp.float32)
    q_sum, merged_all = lax.scan(second_pass, q_start, (group_rows, grad_all, group_resid, group_ids))
    q_new = q_sum / N_DP

    def third_pass(inputs):
        merged_here, ids_here = inputs
        outputs = []
        for block in range(KBLK):
            first_row = (ids_here[block] * BLK).astype(jnp.int32)
            p_rows = lax.dynamic_slice_in_dim(p_flat, first_row, BLK, 0)
            approx = jnp.einsum('bmr,mcr->bmc', p_rows.reshape(BLK, N_MP, RANK), q_new, precision=HIGHEST_PRECISION).reshape(BLK, KVW)
            outputs.append(merged_here[block] - approx)
        return jnp.stack(outputs)
    new_resid = lax.map(third_pass, (merged_all, group_ids))
    return (p_flat, q_new.reshape(KVW, RANK), new_resid.reshape(N_DP * KBLK, BLK, KVW))
```

```python
import functools
import jax
import jax.numpy as jnp
from jax import lax
from jax.experimental import pallas as pl
from jax.experimental.pallas import tpu as pltpu
from jax.sharding import PartitionSpec as P

F32 = jnp.float32
BF16 = jnp.bfloat16
HIGHEST = lax.Precision.HIGHEST
VMEM_LIMIT = 48 * 1024 * 1024


def packed_tables(lengths, assign, rewards, slot_count, capacity):
    groups, sequences = lengths.shape
    offsets = jnp.cumsum(lengths, axis=1) - lengths
    advantage = rewards - jnp.mean(rewards, axis=1, keepdims=True)
    seq_weight = advantage / lengths.astype(rewards.dtype)
    positions = jnp.arange(slot_count)
    seq_index = jnp.arange(sequences)
    inside = (offsets[:, None, :] <= positions[None, :, None]).astype(jnp.int32)
    owner = jnp.sum(inside, axis=2) - 1
    picked = owner[:, :, None] == seq_index[None, None, :]
    seq_start = jnp.sum(jnp.where(picked, offsets[:, None, :], 0), axis=2)
    learner = jnp.sum(jnp.where(picked, assign[:, None, :], 0), axis=2)
    row_weight = jnp.sum(jnp.where(picked, seq_weight[:, None, :], 0.0), axis=2)
    source = jnp.arange(groups)[:, None]
    slot_table = learner * (groups * capacity) + source * capacity + positions[None, :] - seq_start
    return (slot_table, row_weight)


def dot(a, b, dims, precision=None):
    return lax.dot_general(a, b, (dims, ((), ())), precision=precision, preferred_element_type=F32)


NN, NT, TN = ((1,), (0,)), ((1,), (1,)), ((0,), (0,))


def split(a, parts):
    out = []
    for _ in range(parts):
        high = a.astype(BF16)
        out.append(high)
        a = a - high.astype(F32)
    return jnp.concatenate(out, axis=0)


def fold(a, parts):
    rows = a.shape[0] // parts
    total = a[:rows]
    for i in range(1, parts):
        total = total + a[i * rows:(i + 1) * rows]
    return total


SMEM = pl.BlockSpec(memory_space=pltpu.SMEM)
VMEM = pl.BlockSpec(memory_space=pltpu.VMEM)


def call(kernel, n_smem, n_vmem, outs, scratch=(), flops=1000000, bytes_accessed=1000000, name=None):
    return pl.pallas_call(
        kernel,
        out_shape=outs,
        in_specs=[SMEM] * n_smem + [VMEM] * n_vmem,
        out_specs=jax.tree.map(lambda _: VMEM, outs),
        scratch_shapes=list(scratch),
        compiler_params=pltpu.CompilerParams(vmem_limit_bytes=VMEM_LIMIT),
        cost_estimate=pl.CostEstimate(flops=flops, bytes_accessed=bytes_accessed, transcendentals=0),
        name=name,
    )


def resid_kernel(q0t, resid, out):
    width = resid.shape[1]
    for k in range(resid.shape[0]):
        out[:, k * width:(k + 1) * width] = dot(q0t[...], resid[k], NT, HIGHEST)


def first_kernel(n_x, sel, ids, place, *refs):
    pieces, refs = refs[:n_x], refs[n_x:]
    w, wups, q0t, ft, xall, g, keep, send, h, pt = refs
    step, last = pl.program_id(0), pl.num_programs(0) - 1
    depth = w.shape[0]

    @pl.when(step == 0)
    def _():
        rows = pieces[0].shape[0]
        for j in range(n_x):
            @pl.when(sel[j] >= 0)
            def _():
                xall[pl.ds(pl.multiple_of(sel[j] * rows, rows), rows), :] = pieces[j][...]
        h[...] = jnp.zeros_like(h)

    h[...] += jnp.dot(xall[:, pl.ds(pl.multiple_of(step * depth, depth), depth)], w[...], preferred_element_type=F32)

    @pl.when(step == last)
    def _():
        tangent = jnp.tanh(h[...])
        grad = (wups[...] * (1.0 - tangent * tangent)).astype(BF16)
        g[...] = grad
        yt = split(dot(q0t[...], grad.astype(F32), NT, HIGHEST), 3)
        wide = 1024
        for i in range(pt.shape[1] // wide):
            at = slice(i * wide, (i + 1) * wide)
            pt[:, at] = fold(dot(yt, xall[:, at], NN), 3)
        block = ft.shape[1] // ids.shape[0]
        for k in range(ids.shape[0]):
            at = pl.ds(pl.multiple_of(ids[k] * block, block), block)
            pt[:, at] += ft[:, k * block:(k + 1) * block]
        write_halves(place, pt, keep, send)


def write_halves(place, pt, keep, send):
    if keep is send:
        keep[...] = pt[...]
        return
    chips, rows = keep.shape[:2]
    for k in range(chips):
        chip = place[0] ^ k
        keep[k] = pt[pl.ds(pl.multiple_of((2 * chip + place[1]) * rows, rows), rows), :]
        send[k] = pt[pl.ds(pl.multiple_of((2 * chip + 1 - place[1]) * rows, rows), rows), :]


def merged_kernel(ids, xall, g, resid, out):
    block = resid.shape[1]
    for k in range(ids.shape[0]):
        at = pl.ds(pl.multiple_of(ids[k] * block, block), block)
        out[k] = dot(xall[:, at], g[...], TN) + resid[k]


def second_kernel(n_p, ids, place, *refs):
    parts, refs = refs[:n_p], refs[n_p:]
    xall, g, resid, pt, gram, ut = refs
    if n_p == 1:
        pt[...] = parts[0][...]
    else:
        rows = parts[0].shape[0]
        for j in range(n_p):
            chip, core = place[0] ^ (j // 2), place[1] ^ (j % 2)
            pt[pl.ds(pl.multiple_of((2 * chip + core) * rows, rows), rows), :] = parts[j][...]
    rank = pt.shape[0]
    ps = split(pt[...], 2)
    both = fold(dot(ps, ps, NT), 2)
    gram[...] = both[:, :rank] + both[:, rank:]
    zt = fold(dot(ps, xall[...], NT), 2)
    total = fold(dot(split(zt, 3), g[...], NN), 3)
    block = resid.shape[1]
    for k in range(ids.shape[0]):
        at = pl.ds(pl.multiple_of(ids[k] * block, block), block)
        total = total + dot(pt[:, at], resid[k], NN, HIGHEST)
    ut[...] = total


def factor_kernel(ids, gram, pt, pft, linv, blocks):
    rank = gram.shape[0]
    row_at = lax.broadcasted_iota(jnp.int32, (rank, rank), 0)
    col_at = lax.broadcasted_iota(jnp.int32, (rank, rank), 1)
    eye = (row_at == col_at).astype(F32)
    aug = jnp.concatenate([gram[...], eye], axis=1)
    below = lax.broadcasted_iota(jnp.int32, (rank, 1), 0)
    scale = jnp.zeros((rank, 1), F32)
    for k in range(rank):
        pivot = aug[k:k + 1, k:k + 1]
        scale = jnp.where(below == k, pivot, scale)
        ratio = jnp.where(below > k, aug[:, k:k + 1] / pivot, 0.0)
        aug = aug - ratio * aug[k:k + 1, :]
    inverse = aug[:, rank:] / jnp.sqrt(scale)
    linv[...] = inverse
    wide = 1024
    for i in range(pt.shape[1] // wide):
        at = slice(i * wide, (i + 1) * wide)
        pft[:, at] = dot(inverse, pt[:, at], NN, HIGHEST)
    block = blocks.shape[1] // ids.shape[0]
    for k in range(ids.shape[0]):
        at = pl.ds(pl.multiple_of(ids[k] * block, block), block)
        blocks[:, k * block:(k + 1) * block] = pft[:, at]


def last_kernel(scale, place, half_own, half_other, linv, blocks, merged, qt, out, ut):
    if half_other is None:
        ut[...] = half_own[...]
    else:
        rows = half_own.shape[0]
        ut[pl.ds(pl.multiple_of(place[1] * rows, rows), rows), :] = half_own[...]
        ut[pl.ds(pl.multiple_of((1 - place[1]) * rows, rows), rows), :] = half_other[...]
    q = dot(linv[...], ut[...], NN, HIGHEST) * scale
    qt[...] = q
    block = merged.shape[1]
    for k in range(merged.shape[0]):
        out[k] = merged[k] - dot(blocks[:, k * block:(k + 1) * block], q, TN, HIGHEST)


def gather_rows(x, groups, at):
    if groups % 2:
        return [lax.all_gather(x, "mp", axis=0, tiled=True)], jnp.zeros((1,), jnp.int32)
    pairs_a = [(i, i ^ 1) for i in range(groups)]
    pairs_b = [(i, i + 1 if i % 2 else i - 1) for i in range(1, groups - 1)]
    even = at % 2 == 0
    pieces, owner = [x], [at]
    from_a, from_b = x, x
    for s in range(1, groups):
        new_a = lax.ppermute(from_b, "mp", pairs_a)
        new_b = lax.ppermute(from_a, "mp", pairs_b) if s < groups - 1 else None
        down, up = at + s, at - s
        pieces.append(new_a)
        owner.append(jnp.where(even, down, up))
        if new_b is not None:
            pieces.append(new_b)
            owner.append(jnp.where(even, up, down))
        from_a, from_b = new_a, new_b
    owner = jnp.stack(owner).astype(jnp.int32)
    return pieces, jnp.where((owner >= 0) & (owner < groups), owner, -1)


def swap(a, bit, size):
    return lax.ppermute(a, "dp", [(i, i ^ bit) for i in range(size)])


def shards(gen_rows, lengths, assign, rewards, upstream, weight, q_init, resid, block_ids):
    groups, replicas = lax.axis_size("mp"), lax.axis_size("dp")
    slot_count, depth = gen_rows.shape
    columns, rank = q_init.shape
    capacity = upstream.shape[0] // (groups * groups)
    kept, block = resid.shape[:2]
    rows = groups * slot_count
    at_dp = lax.axis_index("dp")
    place = jnp.stack([at_dp // 2, at_dp % 2]).astype(jnp.int32)
    direct = replicas == 8

    pieces, owner = gather_rows(gen_rows, groups, lax.axis_index("mp"))
    slot_table, row_weight = packed_tables(lengths, assign, rewards, slot_count, capacity)
    upstream_rows = jnp.take(upstream, slot_table.reshape(-1), axis=0)
    weighted = row_weight.reshape(-1)[:, None] * upstream_rows.astype(F32)
    q0t = q_init.T
    shape = jax.ShapeDtypeStruct
    ft = call(resid_kernel, 0, 2, shape((rank, kept * block), F32), name="resid_term")(q0t, resid)

    steps = 5
    n_x = len(pieces)
    full = lambda *dims: pl.BlockSpec(dims, lambda i: (0,) * len(dims))
    if direct:
        chips = replicas // 2
        part = rank // replicas
        halves = [shape((chips, part, depth), F32)] * 2
        kernel = functools.partial(first_kernel, n_x)
    else:
        halves = [shape((rank, depth), F32)]

        def kernel(*refs):
            first_kernel(n_x, *refs[:-2], refs[-3], *refs[-2:])
    xall, g, *halves = pl.pallas_call(
        kernel,
        out_shape=[shape((rows, depth), BF16), shape((rows, columns), BF16)] + halves,
        grid=(steps,),
        in_specs=[SMEM] * 3
        + [full(*p.shape) for p in pieces]
        + [pl.BlockSpec((depth // steps, columns), lambda i: (i, 0))]
        + [full(rows, columns), full(rank, columns), full(rank, kept * block)],
        out_specs=[full(rows, depth), full(rows, columns)] + [full(*s.shape) for s in halves],
        scratch_shapes=[pltpu.VMEM((rows, columns), F32), pltpu.VMEM((rank, depth), F32)],
        compiler_params=pltpu.CompilerParams(vmem_limit_bytes=VMEM_LIMIT),
        cost_estimate=pl.CostEstimate(flops=2 * rows * depth * columns, bytes_accessed=10000000, transcendentals=0),
        name="first",
    )(owner, block_ids, place, *pieces, weight, weighted, q0t, ft)

    merged = call(merged_kernel, 1, 3, shape((kept, block, columns), F32), name="merged")(block_ids, xall, g, resid)

    if direct:
        keep, send = halves
        back = swap(send, 1, replicas)
        sums = [keep[k] + back[k] for k in range(chips)]
        own = sums[0]
        for k in range(1, chips):
            own = own + swap(sums[k], 2 * k, replicas)
        same = [own] + [swap(own, 2 * k, replicas) for k in range(1, chips)]
        p_parts = []
        for s in same:
            p_parts += [s, swap(s, 1, replicas)]
    else:
        p_parts = [lax.psum(halves[0], "dp")]

    n_p = len(p_parts)
    pt, gram, ut = call(
        functools.partial(second_kernel, n_p), 2, n_p + 3,
        [shape((rank, depth), F32), shape((rank, rank), F32), shape((rank, columns), F32)], name="second",
    )(block_ids, place, *p_parts, xall, g, resid)

    pft, linv, blocks = call(
        factor_kernel, 1, 2,
        [shape((rank, depth), F32), shape((rank, rank), F32), shape((rank, kept * block), F32)], name="factor",
    )(block_ids, gram, pt)

    if direct:
        half = rank // 2
        mine = lax.dynamic_slice_in_dim(ut, place[1] * half, half, 0)
        other = lax.dynamic_slice_in_dim(ut, (1 - place[1]) * half, half, 0)
        chip_sum = mine + swap(other, 1, replicas)
        total = chip_sum
        for k in range(1, chips):
            total = total + swap(chip_sum, 2 * k, replicas)
        u_parts = [total, swap(total, 1, replicas)]
        tail = functools.partial(last_kernel, 1.0 / replicas)
    else:
        u_parts = [lax.psum(ut, "dp")]

        def tail(place, half_own, *refs):
            last_kernel(1.0 / replicas, place, half_own, None, *refs)
    qt, new_resid = call(
        tail, 1, len(u_parts) + 3,
        [shape((rank, columns), F32), shape((kept, block, columns), F32)],
        [pltpu.VMEM((rank, columns), F32)], name="last",
    )(place, *u_parts, linv, blocks, merged)
    return pft.T, qt.T, new_resid


def solution(mesh):
    placed = (
        P(("dp", "mp"), None),
        P("dp", None),
        P("dp", None),
        P("dp", None),
        P("dp", "mp"),
        P(None, "mp"),
        P("mp", None),
        P("dp", None, "mp"),
        P("dp"),
    )
    return jax.shard_map(
        shards,
        mesh=mesh,
        in_specs=placed,
        out_specs=(P(None, "mp"), P("mp", None), P("dp", None, "mp")),
        check_vma=False,
    )
```

```python
import functools
import jax
import jax.numpy as jnp
from jax import lax
from jax.experimental import pallas as pl
from jax.experimental.pallas import tpu as pltpu
from jax.sharding import PartitionSpec as P

F32 = jnp.float32
BF16 = jnp.bfloat16
HIGHEST = lax.Precision.HIGHEST
VMEM_LIMIT = 16 * 1024 * 1024


def packed_tables(lengths, assign, rewards, order, slot_count, capacity):
    groups, sequences = lengths.shape
    lengths, assign, rewards = lengths[order], assign[order], rewards[order]
    offsets = jnp.cumsum(lengths, axis=1) - lengths
    advantage = rewards - jnp.mean(rewards, axis=1, keepdims=True)
    seq_weight = advantage / lengths.astype(rewards.dtype)
    positions = jnp.arange(slot_count)
    seq_index = jnp.arange(sequences)
    inside = (offsets[:, None, :] <= positions[None, :, None]).astype(jnp.int32)
    owner = jnp.sum(inside, axis=2) - 1
    picked = owner[:, :, None] == seq_index[None, None, :]
    seq_start = jnp.sum(jnp.where(picked, offsets[:, None, :], 0), axis=2)
    learner = jnp.sum(jnp.where(picked, assign[:, None, :], 0), axis=2)
    row_weight = jnp.sum(jnp.where(picked, seq_weight[:, None, :], 0.0), axis=2)
    source = order[:, None]
    slot_table = learner * (groups * capacity) + source * capacity + positions[None, :] - seq_start
    return (slot_table, row_weight)


def dot(a, b, dims, precision=None):
    return lax.dot_general(a, b, (dims, ((), ())), precision=precision, preferred_element_type=F32)


NN, NT, TN = ((1,), (0,)), ((1,), (1,)), ((0,), (0,))
SMEM = pl.BlockSpec(memory_space=pltpu.SMEM)
VMEM = pl.BlockSpec(memory_space=pltpu.VMEM)


def split(a, parts):
    out = []
    for _ in range(parts):
        high = a.astype(BF16)
        out.append(high)
        a = a - high.astype(F32)
    return jnp.concatenate(out, axis=0)


def fold(a, parts):
    rows = a.shape[0] // parts
    total = a[:rows]
    for i in range(1, parts):
        total = total + a[i * rows:(i + 1) * rows]
    return total


def lanes(index, width):
    return pl.ds(pl.multiple_of(index * width, width), width)


def call(kernel, n_smem, n_vmem, outs, scratch=(), flops=1000000, name=None):
    return pl.pallas_call(
        kernel,
        out_shape=outs,
        in_specs=[SMEM] * n_smem + [VMEM] * n_vmem,
        out_specs=jax.tree.map(lambda _: VMEM, outs),
        scratch_shapes=list(scratch),
        compiler_params=pltpu.CompilerParams(vmem_limit_bytes=VMEM_LIMIT),
        cost_estimate=pl.CostEstimate(flops=flops, bytes_accessed=1000000, transcendentals=0),
        name=name,
    )


def resid_kernel(q0t, resid, q3, ft, r2):
    q3[...] = split(q0t[...], 3)
    kept, width = resid.shape[:2]
    for k in range(kept):
        ft[:, k * width:(k + 1) * width] = dot(q0t[...], resid[k], NT, HIGHEST)
        high = resid[k].astype(BF16)
        r2[0, k * width:(k + 1) * width, :] = high
        r2[1, k * width:(k + 1) * width, :] = (resid[k] - high.astype(F32)).astype(BF16)


def pick(pieces, flag, choices, at, out):
    rows = out.shape[0] // len(choices)
    for j, (first, second) in enumerate(choices):
        here = slice(j * rows, (j + 1) * rows)
        if second is None:
            out[here, :] = pieces[first][...]
        else:
            @pl.when(flag[0] == 1)
            def _():
                out[here, :] = pieces[first][...]

            @pl.when(flag[0] == 0)
            def _():
                out[here, :] = pieces[second][...]


def row_grad(x, w, weighted, q3, g):
    tangent = jnp.tanh(jnp.dot(x[...], w[...], preferred_element_type=F32))
    grad = (weighted[...] * (1.0 - tangent * tangent)).astype(BF16)
    g[...] = grad
    return split(fold(dot(q3[...], grad, NT), 3), 3)


def stage_kernel(n_x, choices, flag, *refs):
    pieces, (w, weighted, q3, x, g, pt) = refs[:n_x], refs[n_x:]
    pick(pieces, flag, choices, 0, x)
    yt = row_grad(x, w, weighted, q3, g)
    wide = 1024
    for i in range(pt.shape[1] // wide):
        at = slice(i * wide, (i + 1) * wide)
        pt[:, at] = fold(dot(yt, x[:, at], NN), 3)


def tail_kernel(n_x, choices, flag, ids, place, *refs):
    pieces, refs = refs[:n_x], refs[n_x:]
    w, weighted, q3, ft, pt0, x, g = refs[:7]
    outs, pt = refs[7:-1], refs[-1]
    pick(pieces, flag, choices, 0, x)
    yt = row_grad(x, w, weighted, q3, g)
    wide = 1024
    for i in range(pt.shape[1] // wide):
        at = slice(i * wide, (i + 1) * wide)
        pt[:, at] = pt0[:, at] + fold(dot(yt, x[:, at], NN), 3)
    block = ft.shape[1] // ids.shape[0]
    for k in range(ids.shape[0]):
        pt[:, lanes(ids[k], block)] += ft[:, k * block:(k + 1) * block]
    if len(outs) == 1:
        outs[0][...] = pt[...]
        return
    for j, out in enumerate(outs):
        chip, core = place[0] ^ (j // 2), place[1] ^ (j % 2)
        out[...] = pt[lanes(2 * chip + core, out.shape[0]), :]


def merged_kernel(ids, xa, xb, ga, gb, resid, out):
    block = resid.shape[1]
    for k in range(ids.shape[0]):
        at = lanes(ids[k], block)
        out[k] = dot(xa[:, at], ga[...], TN) + dot(xb[:, at], gb[...], TN) + resid[k]


def second_kernel(n_p, ids, place, *refs):
    parts, refs = refs[:n_p], refs[n_p:]
    xa, xb, ga, gb, r2 = refs[:5]
    ps, gram = refs[5:7]
    uts, pt, pk = refs[7:-2], refs[-2], refs[-1]
    if n_p == 1:
        pt[...] = parts[0][...]
    else:
        rows = parts[0].shape[0]
        for j in range(n_p):
            chip, core = place[0] ^ (j // 2), place[1] ^ (j % 2)
            pt[lanes(2 * chip + core, rows), :] = parts[j][...]
    rank = pt.shape[0]
    two = split(pt[...], 2)
    ps[...] = two
    block = pk.shape[1] // ids.shape[0]
    for k in range(ids.shape[0]):
        pk[:, k * block:(k + 1) * block] = ps[:, lanes(ids[k], block)]
    both = fold(dot(two, two, NT), 2)
    gram[...] = both[:, :rank] + both[:, rank:]
    za = split(fold(dot(two, xa[...], NT), 2), 3)
    zb = split(fold(dot(two, xb[...], NT), 2), 3)
    total = fold(dot(za, ga[...], NN) + dot(zb, gb[...], NN), 3)
    total = total + fold(dot(pk[...], r2[0], NN), 2) + dot(pk[:rank, :], r2[1], NN)
    if len(uts) == 1:
        uts[0][...] = total
    else:
        half = rank // 2
        low_is_mine = place[1] == 0
        uts[0][...] = jnp.where(low_is_mine, total[:half], total[half:])
        uts[1][...] = jnp.where(low_is_mine, total[half:], total[:half])


def factor_kernel(ids, gram, ps, pft, linv, blocks):
    rank = gram.shape[0]
    sub = 8
    eye = (lax.broadcasted_iota(jnp.int32, (rank, rank), 0) == lax.broadcasted_iota(jnp.int32, (rank, rank), 1)).astype(F32)
    aug = jnp.concatenate([gram[...], eye], axis=1)
    rows = [aug[b * sub:(b + 1) * sub] for b in range(rank // sub)]
    place = lax.broadcasted_iota(jnp.int32, (sub, 1), 0)
    for k in range(rank):
        b, r = k // sub, k % sub
        row = rows[b][r:r + 1, :]
        pivot = row[:, k:k + 1]
        linv[k:k + 1, :] = (row / jnp.sqrt(pivot))[:, rank:]
        ratio = row / pivot
        if r < sub - 1:
            rows[b] = rows[b] - jnp.where(place > r, rows[b][:, k:k + 1], 0.0) * ratio
        for c in range(b + 1, rank // sub):
            rows[c] = rows[c] - rows[c][:, k:k + 1] * ratio
    inverse = linv[...]
    high = inverse.astype(BF16)
    low = (inverse - high.astype(F32)).astype(BF16)
    lhs = jnp.concatenate([jnp.concatenate([high, high], axis=1), jnp.concatenate([low, jnp.zeros_like(low)], axis=1)], axis=0)
    wide = 1024
    for i in range(pft.shape[1] // wide):
        at = slice(i * wide, (i + 1) * wide)
        pft[:, at] = fold(dot(lhs, ps[:, at], NN), 2)
    block = blocks.shape[1] // ids.shape[0]
    for k in range(ids.shape[0]):
        piece = pft[:, lanes(ids[k], block)]
        two = split(piece, 2)
        at = slice(k * block, (k + 1) * block)
        blocks[:2 * rank, at] = two
        blocks[2 * rank:, at] = two[:rank]


def last_kernel(n_u, scale, place, *refs):
    halves, (linv, blocks, merged, qt, out, ut) = refs[:n_u], refs[n_u:]
    if n_u == 1:
        ut[...] = halves[0][...]
    else:
        rows = halves[0].shape[0]
        ut[lanes(place[1], rows), :] = halves[0][...]
        ut[lanes(1 - place[1], rows), :] = halves[1][...]
    q = dot(linv[...], ut[...], NN, HIGHEST) * scale
    qt[...] = q
    two = split(q, 2)
    rank = q.shape[0]
    rhs = jnp.concatenate([two[:rank], two[:rank], two[rank:]], axis=0)
    block = merged.shape[1]
    for k in range(merged.shape[0]):
        out[k] = merged[k] - dot(blocks[:, k * block:(k + 1) * block], rhs, TN)


def gather_rows(x, groups, at):
    if groups != 4:
        rows = x.shape[0]
        whole = lax.all_gather(x, "mp", axis=0, tiled=True)
        pieces = [whole[j * rows:(j + 1) * rows] for j in range(groups)]
        return pieces, [(j, None) for j in range(groups)], jnp.zeros((1,), jnp.int32), jnp.arange(groups)
    outer = [(0, 1), (1, 0), (2, 3), (3, 2)]
    inner = [(1, 2), (2, 1)]
    a0 = lax.ppermute(x, "mp", outer)
    b0 = lax.ppermute(x, "mp", inner)
    b1 = lax.ppermute(a0, "mp", inner)
    a1 = lax.ppermute(b0, "mp", outer)
    a2 = lax.ppermute(b1, "mp", outer)
    at_end = (at == 0) | (at == 3)
    low = at < 2
    order = jnp.stack([at, at ^ 1, jnp.where(low, 2, 1), jnp.where(low, 3, 0)])
    choices = [(0, None), (1, None), (2, 3), (4, 5)]
    return [x, a0, a1, b0, a2, b1], choices, at_end.astype(jnp.int32).reshape(1), order


def swap(a, bit, size):
    return lax.ppermute(a, "dp", [(i, i ^ bit) for i in range(size)])


def together(*values):
    return lax.optimization_barrier(values)


def shards(gen_rows, lengths, assign, rewards, upstream, weight, q_init, resid, block_ids):
    groups, replicas = lax.axis_size("mp"), lax.axis_size("dp")
    slot_count, depth = gen_rows.shape
    columns, rank = q_init.shape
    capacity = upstream.shape[0] // (groups * groups)
    kept, block = resid.shape[:2]
    at_dp = lax.axis_index("dp")
    place = jnp.stack([at_dp // 2, at_dp % 2]).astype(jnp.int32)
    direct = replicas == 8
    shape = jax.ShapeDtypeStruct

    pieces, choices, flag, order = gather_rows(gen_rows, groups, lax.axis_index("mp"))
    slot_table, row_weight = packed_tables(lengths, assign, rewards, order, slot_count, capacity)
    upstream_rows = jnp.take(upstream, slot_table.reshape(-1), axis=0)
    weighted = row_weight.reshape(-1)[:, None] * upstream_rows.astype(F32)
    q3, ft, r2 = call(
        resid_kernel, 0, 2,
        [shape((3 * rank, columns), BF16), shape((rank, kept * block), F32), shape((2, kept * block, columns), BF16)],
        name="resid_term",
    )(q_init.T, resid)

    early_rows = (groups - 1) * slot_count
    n_early = choices[-2][1] + 1 if choices[-2][1] is not None else choices[-2][0] + 1
    early, late = pieces[:n_early], pieces[n_early:]
    xa, ga, pt0 = call(
        functools.partial(stage_kernel, len(early), choices[:-1]), 1, len(early) + 3,
        [shape((early_rows, depth), BF16), shape((early_rows, columns), BF16), shape((rank, depth), F32)],
        flops=2 * early_rows * depth * columns, name="stage",
    )(flag, *early, weight, weighted[:early_rows], q3)

    late_choices = [(0, 1 if len(late) == 2 else None)]
    if direct:
        outs = [shape((rank // replicas, depth), F32)] * replicas
    else:
        outs = [shape((rank, depth), F32)]
    xb, gb, *parts = call(
        functools.partial(tail_kernel, len(late), late_choices), 3, len(late) + 5,
        [shape((slot_count, depth), BF16), shape((slot_count, columns), BF16)] + outs,
        [pltpu.VMEM((rank, depth), F32)],
        flops=2 * slot_count * depth * columns, name="tail",
    )(flag, block_ids, place, *late, weight, weighted[early_rows:], q3, ft, pt0)

    merged = call(merged_kernel, 1, 5, shape((kept, block, columns), F32), name="merged")(block_ids, xa, xb, ga, gb, resid)

    if direct:
        chips = replicas // 2
        sums = [parts[2 * k] + swap(parts[2 * k + 1], 1, replicas) for k in range(chips)]
        got = [swap(sums[k], 2 * k, replicas) for k in range(1, chips)]
        *got, merged = together(*got, merged)
        own = sums[0] + got[0] + got[1] + got[2]
        same = [own] + [swap(own, 2 * k, replicas) for k in range(1, chips)]
        p_parts = []
        for s in same:
            p_parts += [s, swap(s, 1, replicas)]
        u_shapes = [shape((rank // 2, columns), F32)] * 2
    else:
        p_parts = [lax.psum(parts[0], "dp")]
        u_shapes = [shape((rank, columns), F32)]

    n_p = len(p_parts)
    ps, gram, *us = call(
        functools.partial(second_kernel, n_p), 2, n_p + 5,
        [shape((2 * rank, depth), BF16), shape((rank, rank), F32)] + u_shapes,
        [pltpu.VMEM((rank, depth), F32), pltpu.VMEM((2 * rank, kept * block), BF16)], name="second",
    )(block_ids, place, *p_parts, xa, xb, ga, gb, r2)

    pft, linv, blocks = call(
        factor_kernel, 1, 2,
        [shape((rank, depth), F32), shape((rank, rank), F32), shape((3 * rank, kept * block), BF16)], name="factor",
    )(block_ids, gram, ps)

    if direct:
        chip_sum = us[0] + swap(us[1], 1, replicas)
        got = [swap(chip_sum, 2 * k, replicas) for k in range(1, chips)]
        *got, linv = together(*got, linv)
        total = chip_sum + got[0] + got[1] + got[2]
        u_parts = [total, swap(total, 1, replicas)]
    else:
        u_parts = [lax.psum(us[0], "dp")]
    n_u = len(u_parts)
    qt, new_resid = call(
        functools.partial(last_kernel, n_u, 1.0 / replicas), 1, n_u + 3,
        [shape((rank, columns), F32), shape((kept, block, columns), F32)],
        [pltpu.VMEM((rank, columns), F32)], name="last",
    )(place, *u_parts, linv, blocks, merged)
    return pft.T, qt.T, new_resid


def solution(mesh):
    placed = (
        P(("dp", "mp"), None),
        P("dp", None),
        P("dp", None),
        P("dp", None),
        P("dp", "mp"),
        P(None, "mp"),
        P("mp", None),
        P("dp", None, "mp"),
        P("dp"),
    )
    return jax.shard_map(
        shards,
        mesh=mesh,
        in_specs=placed,
        out_specs=(P(None, "mp"), P("mp", None), P("dp", None, "mp")),
        check_vma=False,
    )
```

```python
import functools
import jax
import jax.numpy as jnp
from jax import lax
from jax.experimental import pallas as pl
from jax.experimental.pallas import tpu as pltpu
from jax.sharding import PartitionSpec as P

F32 = jnp.float32
BF16 = jnp.bfloat16
HIGHEST = lax.Precision.HIGHEST
VMEM_LIMIT = 16 * 1024 * 1024


def packed_tables(lengths, assign, rewards, order, slot_count, capacity):
    groups, sequences = lengths.shape
    lengths, assign, rewards = lengths[order], assign[order], rewards[order]
    offsets = jnp.cumsum(lengths, axis=1) - lengths
    advantage = rewards - jnp.mean(rewards, axis=1, keepdims=True)
    seq_weight = advantage / lengths.astype(rewards.dtype)
    positions = jnp.arange(slot_count)
    seq_index = jnp.arange(sequences)
    inside = (offsets[:, None, :] <= positions[None, :, None]).astype(jnp.int32)
    owner = jnp.sum(inside, axis=2) - 1
    picked = owner[:, :, None] == seq_index[None, None, :]
    seq_start = jnp.sum(jnp.where(picked, offsets[:, None, :], 0), axis=2)
    learner = jnp.sum(jnp.where(picked, assign[:, None, :], 0), axis=2)
    row_weight = jnp.sum(jnp.where(picked, seq_weight[:, None, :], 0.0), axis=2)
    source = order[:, None]
    slot_table = learner * (groups * capacity) + source * capacity + positions[None, :] - seq_start
    return (slot_table, row_weight)


def dot(a, b, dims, precision=None):
    return lax.dot_general(a, b, (dims, ((), ())), precision=precision, preferred_element_type=F32)


NN, NT, TN = ((1,), (0,)), ((1,), (1,)), ((0,), (0,))
SMEM = pl.BlockSpec(memory_space=pltpu.SMEM)
VMEM = pl.BlockSpec(memory_space=pltpu.VMEM)


def split(a, parts):
    out = []
    for _ in range(parts):
        high = a.astype(BF16)
        out.append(high)
        a = a - high.astype(F32)
    return jnp.concatenate(out, axis=0)


def fold(a, parts):
    rows = a.shape[0] // parts
    total = a[:rows]
    for i in range(1, parts):
        total = total + a[i * rows:(i + 1) * rows]
    return total


def lanes(index, width):
    return pl.ds(pl.multiple_of(index * width, width), width)


def call(kernel, n_smem, n_vmem, outs, scratch=(), flops=1000000, name=None, aliases=None):
    return pl.pallas_call(
        kernel,
        input_output_aliases=aliases or {},
        out_shape=outs,
        in_specs=[SMEM] * n_smem + [VMEM] * n_vmem,
        out_specs=jax.tree.map(lambda _: VMEM, outs),
        scratch_shapes=list(scratch),
        compiler_params=pltpu.CompilerParams(vmem_limit_bytes=VMEM_LIMIT),
        cost_estimate=pl.CostEstimate(flops=flops, bytes_accessed=1000000, transcendentals=0),
        name=name,
    )


def resid_kernel(q0t, resid, q3, ft, r2):
    q3[...] = split(q0t[...], 3)
    kept, width = resid.shape[:2]
    for k in range(kept):
        ft[:, k * width:(k + 1) * width] = dot(q0t[...], resid[k], NT, HIGHEST)
        high = resid[k].astype(BF16)
        r2[0, k * width:(k + 1) * width, :] = high
        r2[1, k * width:(k + 1) * width, :] = (resid[k] - high.astype(F32)).astype(BF16)


def pick(pieces, flag, choices, out):
    rows = out.shape[0] // len(choices)
    for j, (first, second) in enumerate(choices):
        here = slice(j * rows, (j + 1) * rows)
        if second is None:
            out[here, :] = pieces[first][...]
        else:
            @pl.when(flag[0] == 1)
            def _():
                out[here, :] = pieces[first][...]

            @pl.when(flag[0] == 0)
            def _():
                out[here, :] = pieces[second][...]


def row_grad(x, w, weighted, q3, g):
    tangent = jnp.tanh(jnp.dot(x[...], w[...], preferred_element_type=F32))
    grad = (weighted[...] * (1.0 - tangent * tangent)).astype(BF16)
    g[...] = grad
    return split(fold(dot(q3[...], grad, NT), 3), 3)


def stage_kernel(n_x, choices, flag, *refs):
    pieces, (w, weighted, q3, bx, g, pt) = refs[:n_x], refs[n_x:]
    x = bx.at[2 * pt.shape[0]:2 * pt.shape[0] + g.shape[0], :]
    pick(pieces, flag, choices, x)
    yt = row_grad(x, w, weighted, q3, g)
    wide = 1024
    for i in range(pt.shape[1] // wide):
        at = slice(i * wide, (i + 1) * wide)
        pt[:, at] = fold(dot(yt, x[:, at], NN), 3)


def tail_kernel(n_x, choices, flag, ids, place, *refs):
    pieces, refs = refs[:n_x], refs[n_x:]
    w, weighted, q3, ft, pt0, _, bx, g = refs[:8]
    outs, pt = refs[8:-1], refs[-1]
    x = bx.at[bx.shape[0] - g.shape[0]:, :]
    pick(pieces, flag, choices, x)
    yt = row_grad(x, w, weighted, q3, g)
    wide = 1024
    for i in range(pt.shape[1] // wide):
        at = slice(i * wide, (i + 1) * wide)
        pt[:, at] = pt0[:, at] + fold(dot(yt, x[:, at], NN), 3)
    block = ft.shape[1] // ids.shape[0]
    for k in range(ids.shape[0]):
        pt[:, lanes(ids[k], block)] += ft[:, k * block:(k + 1) * block]
    if len(outs) == 1:
        outs[0][...] = pt[...]
        return
    for j, out in enumerate(outs):
        chip, core = place[0] ^ (j // 2), place[1] ^ (j % 2)
        out[...] = pt[lanes(2 * chip + core, out.shape[0]), :]


def merged_kernel(ids, bx, ga, gb, resid, out):
    block = resid.shape[1]
    late = gb.shape[0]
    early = ga.shape[0]
    end = bx.shape[0]
    for k in range(ids.shape[0]):
        at = lanes(ids[k], block)
        out[k] = dot(bx[end - early - late:end - late, at], ga[...], TN) + dot(bx[end - late:, at], gb[...], TN) + resid[k]


def second_kernel(n_p, ids, place, *refs):
    parts, refs = refs[:n_p], refs[n_p:]
    ga, gb, r2, _, bx, gram = refs[:6]
    uts, pk = refs[6:-1], refs[-1]
    rank = pk.shape[0] // 2
    if n_p == 1:
        bx[:2 * rank, :] = split(parts[0][...], 2)
    else:
        rows = parts[0].shape[0]
        for j in range(0, n_p, 2):
            chip = place[0] ^ (j // 2)
            swapped = place[1] == 1
            first, second = parts[j][...], parts[j + 1][...]
            pair = jnp.concatenate([jnp.where(swapped, second, first), jnp.where(swapped, first, second)], axis=0)
            high = pair.astype(BF16)
            bx[lanes(chip, 2 * rows), :] = high
            bx[pl.ds(pl.multiple_of(rank + chip * 2 * rows, 2 * rows), 2 * rows), :] = (pair - high.astype(F32)).astype(BF16)
    block = pk.shape[1] // ids.shape[0]
    for k in range(ids.shape[0]):
        pk[:, k * block:(k + 1) * block] = bx[:2 * rank, lanes(ids[k], block)]
    both = fold(dot(bx[:2 * rank, :], bx[...], NT), 2)
    gram[...] = both[:, :rank] + both[:, rank:2 * rank]
    early = ga.shape[0]
    zt = split(both[:, 2 * rank:], 3)
    total = fold(dot(zt[:, :early], ga[...], NN) + dot(zt[:, early:], gb[...], NN), 3)
    total = total + fold(dot(pk[...], r2[0], NN), 2) + dot(pk[:rank, :], r2[1], NN)
    if len(uts) == 1:
        uts[0][...] = total
    else:
        half = rank // 2
        low_is_mine = place[1] == 0
        uts[0][...] = jnp.where(low_is_mine, total[:half], total[half:])
        uts[1][...] = jnp.where(low_is_mine, total[half:], total[:half])


def inverse_factor(gram):
    rank, sub = gram.shape[0], 8
    blocks = rank // sub
    eye = (lax.broadcasted_iota(jnp.int32, (rank, rank), 0) == lax.broadcasted_iota(jnp.int32, (rank, rank), 1)).astype(F32)
    whole = jnp.concatenate([gram, eye], axis=1)
    rows = [whole[b * sub:(b + 1) * sub] for b in range(blocks)]
    place = lax.broadcasted_iota(jnp.int32, (sub, 2 * rank), 0)

    def column(a, k):
        return jnp.take_along_axis(a, jnp.full(a.shape, k, jnp.int32), axis=1)

    out = []
    for b in range(blocks):
        panel = rows[b]
        entry = [column(panel, b * sub + j) for j in range(sub)]
        pivots = jnp.zeros_like(panel)
        scale = []
        for i in range(sub):
            scale.append(1.0 / entry[i][i:i + 1, :])
            pivots = jnp.where(place == i, entry[i], pivots)
            ratio = jnp.where(place > i, entry[i], 0.0) * scale[i]
            panel = panel - ratio * panel[i:i + 1, :]
            for j in range(i + 1, sub):
                entry[j] = entry[j] - ratio * entry[j][i:i + 1, :]
        out.append((panel / jnp.sqrt(pivots))[:, rank:])
        solved = [panel[i:i + 1, :] * scale[i] for i in range(sub)]
        for i in range(sub - 1, -1, -1):
            for j in range(i + 1, sub):
                solved[i] = solved[i] - (entry[j][i:i + 1, :] * scale[i]) * solved[j]
        for c in range(b + 1, blocks):
            update = column(rows[c], b * sub) * solved[0]
            for j in range(1, sub):
                update = update + column(rows[c], b * sub + j) * solved[j]
            rows[c] = rows[c] - update
    return jnp.concatenate(out, axis=0)


def factor_kernel(ids, gram, bx, pft, linv, blocks):
    rank = gram.shape[0]
    inverse = inverse_factor(gram[...])
    linv[...] = inverse
    high = inverse.astype(BF16)
    low = (inverse - high.astype(F32)).astype(BF16)
    lhs = jnp.concatenate([jnp.concatenate([high, high], axis=1), jnp.concatenate([low, jnp.zeros_like(low)], axis=1)], axis=0)
    wide = 1024
    for i in range(pft.shape[1] // wide):
        at = slice(i * wide, (i + 1) * wide)
        pft[:, at] = fold(dot(lhs, bx[:2 * rank, at], NN), 2)
    block = blocks.shape[0] // ids.shape[0]
    for k in range(ids.shape[0]):
        piece = jnp.transpose(pft[:, lanes(ids[k], block)])
        high = piece.astype(BF16)
        low = (piece - high.astype(F32)).astype(BF16)
        blocks[k * block:(k + 1) * block, :] = jnp.concatenate([high, low, high], axis=1)


def last_kernel(n_u, scale, place, *refs):
    halves, (linv, blocks, merged, qt, out, ut) = refs[:n_u], refs[n_u:]
    if n_u == 1:
        ut[...] = halves[0][...]
    else:
        rows = halves[0].shape[0]
        ut[lanes(place[1], rows), :] = halves[0][...]
        ut[lanes(1 - place[1], rows), :] = halves[1][...]
    q = dot(linv[...], ut[...], NN, HIGHEST) * scale
    qt[...] = q
    two = split(q, 2)
    rank = q.shape[0]
    rhs = jnp.concatenate([two[:rank], two[:rank], two[rank:]], axis=0)
    block = merged.shape[1]
    for k in range(merged.shape[0]):
        out[k] = merged[k] - dot(blocks[k * block:(k + 1) * block, :], rhs, NN)


def gather_rows(x, groups, at):
    if groups != 4:
        rows = x.shape[0]
        whole = lax.all_gather(x, "mp", axis=0, tiled=True)
        pieces = [whole[j * rows:(j + 1) * rows] for j in range(groups)]
        return pieces, [(j, None) for j in range(groups)], jnp.zeros((1,), jnp.int32), jnp.arange(groups)
    outer = [(0, 1), (1, 0), (2, 3), (3, 2)]
    inner = [(1, 2), (2, 1)]
    a0 = lax.ppermute(x, "mp", outer)
    b0 = lax.ppermute(x, "mp", inner)
    b1 = lax.ppermute(a0, "mp", inner)
    a1 = lax.ppermute(b0, "mp", outer)
    a2 = lax.ppermute(b1, "mp", outer)
    at_end = (at == 0) | (at == 3)
    low = at < 2
    order = jnp.stack([at, at ^ 1, jnp.where(low, 2, 1), jnp.where(low, 3, 0)])
    choices = [(0, None), (1, None), (2, 3), (4, 5)]
    return [x, a0, a1, b0, a2, b1], choices, at_end.astype(jnp.int32).reshape(1), order


def swap(a, bit, size):
    return lax.ppermute(a, "dp", [(i, i ^ bit) for i in range(size)])


def together(*values):
    return lax.optimization_barrier(values)


def shards(gen_rows, lengths, assign, rewards, upstream, weight, q_init, resid, block_ids):
    groups, replicas = lax.axis_size("mp"), lax.axis_size("dp")
    slot_count, depth = gen_rows.shape
    columns, rank = q_init.shape
    capacity = upstream.shape[0] // (groups * groups)
    kept, block = resid.shape[:2]
    at_dp = lax.axis_index("dp")
    place = jnp.stack([at_dp // 2, at_dp % 2]).astype(jnp.int32)
    direct = replicas == 8
    shape = jax.ShapeDtypeStruct

    pieces, choices, flag, order = gather_rows(gen_rows, groups, lax.axis_index("mp"))
    slot_table, row_weight = packed_tables(lengths, assign, rewards, order, slot_count, capacity)
    upstream_rows = jnp.take(upstream, slot_table.reshape(-1), axis=0)
    weighted = row_weight.reshape(-1)[:, None] * upstream_rows.astype(F32)
    q3, ft, r2 = call(
        resid_kernel, 0, 2,
        [shape((3 * rank, columns), BF16), shape((rank, kept * block), F32), shape((2, kept * block, columns), BF16)],
        name="resid_term",
    )(q_init.T, resid)

    early_rows = (groups - 1) * slot_count
    n_early = choices[-2][1] + 1 if choices[-2][1] is not None else choices[-2][0] + 1
    early, late = pieces[:n_early], pieces[n_early:]
    wide_rows = 2 * rank + groups * slot_count
    bx, ga, pt0 = call(
        functools.partial(stage_kernel, len(early), choices[:-1]), 1, len(early) + 3,
        [shape((wide_rows, depth), BF16), shape((early_rows, columns), BF16), shape((rank, depth), F32)],
        flops=2 * early_rows * depth * columns, name="stage",
    )(flag, *early, weight, weighted[:early_rows], q3)

    late_choices = [(0, 1 if len(late) == 2 else None)]
    if direct:
        outs = [shape((rank // replicas, depth), F32)] * replicas
    else:
        outs = [shape((rank, depth), F32)]
    bx, gb, *parts = call(
        functools.partial(tail_kernel, len(late), late_choices), 3, len(late) + 6,
        [shape((wide_rows, depth), BF16), shape((slot_count, columns), BF16)] + outs,
        [pltpu.VMEM((rank, depth), F32)],
        flops=2 * slot_count * depth * columns, name="tail", aliases={len(late) + 8: 0},
    )(flag, block_ids, place, *late, weight, weighted[early_rows:], q3, ft, pt0, bx)

    merged = call(merged_kernel, 1, 4, shape((kept, block, columns), F32), name="merged")(block_ids, bx, ga, gb, resid)

    if direct:
        chips = replicas // 2
        sums = [parts[2 * k] + swap(parts[2 * k + 1], 1, replicas) for k in range(chips)]
        got = [swap(sums[k], 2 * k, replicas) for k in range(1, chips)]
        *got, merged = together(*got, merged)
        own = sums[0] + got[0] + got[1] + got[2]
        same = [own] + [swap(own, 2 * k, replicas) for k in range(1, chips)]
        p_parts = []
        for s in same:
            p_parts += [s, swap(s, 1, replicas)]
        u_shapes = [shape((rank // 2, columns), F32)] * 2
    else:
        p_parts = [lax.psum(parts[0], "dp")]
        u_shapes = [shape((rank, columns), F32)]

    n_p = len(p_parts)
    bx, gram, *us = call(
        functools.partial(second_kernel, n_p), 2, n_p + 4,
        [shape((wide_rows, depth), BF16), shape((rank, rank), F32)] + u_shapes,
        [pltpu.VMEM((2 * rank, kept * block), BF16)], name="second", aliases={n_p + 5: 0},
    )(block_ids, place, *p_parts, ga, gb, r2, bx)

    pft, linv, blocks = call(
        factor_kernel, 1, 2,
        [shape((rank, depth), F32), shape((rank, rank), F32), shape((kept * block, 3 * rank), BF16)], name="factor",
    )(block_ids, gram, bx)

    if direct:
        chip_sum = us[0] + swap(us[1], 1, replicas)
        got = [swap(chip_sum, 2 * k, replicas) for k in range(1, chips)]
        *got, linv = together(*got, linv)
        total = chip_sum + got[0] + got[1] + got[2]
        u_parts = [total, swap(total, 1, replicas)]
    else:
        u_parts = [lax.psum(us[0], "dp")]
    n_u = len(u_parts)
    qt, new_resid = call(
        functools.partial(last_kernel, n_u, 1.0 / replicas), 1, n_u + 3,
        [shape((rank, columns), F32), shape((kept, block, columns), F32)],
        [pltpu.VMEM((rank, columns), F32)], name="last",
    )(place, *u_parts, linv, blocks, merged)
    return pft.T, qt.T, new_resid


def solution(mesh):
    placed = (
        P(("dp", "mp"), None),
        P("dp", None),
        P("dp", None),
        P("dp", None),
        P("dp", "mp"),
        P(None, "mp"),
        P("mp", None),
        P("dp", None, "mp"),
        P("dp"),
    )
    return jax.shard_map(
        shards,
        mesh=mesh,
        in_specs=placed,
        out_specs=(P(None, "mp"), P("mp", None), P("dp", None, "mp")),
        check_vma=False,
    )
```

```python
import functools
import jax
import jax.numpy as jnp
from jax import lax
from jax.experimental import pallas as pl
from jax.experimental.pallas import tpu as pltpu
from jax.sharding import PartitionSpec as P

F32 = jnp.float32
BF16 = jnp.bfloat16
HIGHEST = lax.Precision.HIGHEST
VMEM_LIMIT = 16 * 1024 * 1024
PREPARE_GRANT = 40 * 1024 * 1024


def dot(a, b, dims, precision=None):
    return lax.dot_general(a, b, (dims, ((), ())), precision=precision, preferred_element_type=F32)


NN, NT, TN = ((1,), (0,)), ((1,), (1,)), ((0,), (0,))
VMEM = pl.BlockSpec(memory_space=pltpu.VMEM)
HBM = pl.BlockSpec(memory_space=pltpu.HBM)


def split(a, parts):
    out = []
    for _ in range(parts):
        high = a.astype(BF16)
        out.append(high)
        a = a - high.astype(F32)
    return jnp.concatenate(out, axis=0)


def fold(a, parts):
    rows = a.shape[0] // parts
    total = a[:rows]
    for i in range(1, parts):
        total = total + a[i * rows:(i + 1) * rows]
    return total


def lanes(index, width):
    return pl.ds(pl.multiple_of(index * width, width), width)


def call(kernel, outs, scratch=(), flops=1000000, name=None, aliases=None, out_specs=None, far=0, grant=VMEM_LIMIT):
    def run(*args):
        return pl.pallas_call(
            kernel,
            input_output_aliases=aliases or {},
            out_shape=outs,
            in_specs=[HBM] * far + [VMEM] * (len(args) - far),
            out_specs=out_specs or jax.tree.map(lambda _: VMEM, outs),
            scratch_shapes=list(scratch),
            compiler_params=pltpu.CompilerParams(vmem_limit_bytes=grant),
            cost_estimate=pl.CostEstimate(flops=flops, bytes_accessed=1000000, transcendentals=0),
            name=name,
        )(*args)

    return run


def pick(pieces, choices, out):
    rows = out.shape[0] // len(choices)
    for j, (first, second) in enumerate(choices):
        here = slice(j * rows, (j + 1) * rows)
        if second is None:
            out[here, :] = pieces[first][...]
        else:
            at = lax.axis_index("mp")
            at_end = (at == 0) | (at == lax.axis_size("mp") - 1)

            @pl.when(at_end)
            def _():
                out[here, :] = pieces[first][...]

            @pl.when(jnp.logical_not(at_end))
            def _():
                out[here, :] = pieces[second][...]


def weigh_rows(lengths, assign, rewards, upstream, order, weighted):
    groups, sequences = lengths.shape
    slots = upstream.shape[0]
    capacity = slots // (groups * groups)
    count = weighted.shape[0] // groups
    row = lax.broadcasted_iota(jnp.int32, (count, slots), 0)
    slot = lax.broadcasted_iota(jnp.int32, (count, slots), 1)
    row_only = lax.broadcasted_iota(jnp.int32, (count, 1), 0)
    for j, source in enumerate(order):
        picked = jnp.zeros((count, slots), jnp.bool_)
        gain, size = jnp.zeros((count, 1), F32), jnp.ones((count, 1), F32)
        total = rewards[source, 0]
        for s in range(1, sequences):
            total = total + rewards[source, s]
        mean = total * (1.0 / sequences)
        offset = jnp.int32(0)
        for s in range(sequences):
            length = lengths[source, s]
            base = assign[source, s] * (groups * capacity) + source * capacity - offset
            inside = (row >= offset) & (row < offset + length)
            picked = picked | (inside & (slot == row + base))
            inside = (row_only >= offset) & (row_only < offset + length)
            gain = jnp.where(inside, rewards[source, s] - mean, gain)
            size = jnp.where(inside, length.astype(F32), size)
            offset = offset + length
        rows = jnp.dot(picked.astype(F32).astype(BF16), upstream[...], preferred_element_type=F32)
        weighted[j * count:(j + 1) * count, :] = gain / size * rows


def gather_order(groups):
    if groups != 4:
        return list(range(groups))
    at = lax.axis_index("mp")
    low = at < 2
    return [at, at ^ 1, jnp.where(low, 2, 1), jnp.where(low, 3, 0)]


def prepare_kernel(parts, own, *refs):
    small, (upstream_far, q0t_far, resid_far, w, x), refs = refs[:4], refs[4:9], refs[9:]
    ids, w_near, resid, bx, weighted, q3, r2, total, ordered, upstream, q0t, lengths, assign, rewards, arrived = refs
    pairs = list(zip(small, (lengths, assign, rewards, ids)))
    pairs += [(upstream_far, upstream), (q0t_far, q0t), (resid_far, resid), (w, w_near)]
    if own:
        first = bx.shape[0] - weighted.shape[0]
        pairs.append((x, bx.at[first:first + x.shape[0], :]))
    copies = [pltpu.make_async_copy(a, b, arrived.at[i]) for i, (a, b) in enumerate(pairs)]
    for copy in copies:
        copy.start()
    for copy in copies[:5]:
        copy.wait()
    weigh_rows(lengths, assign, rewards, upstream, gather_order(lengths.shape[0]), weighted)
    copies[5].wait()
    rows, me = ordered.shape[0] // parts, lax.axis_index("dp")
    for j in range(parts):
        ordered[j * rows:(j + 1) * rows, :] = q0t[lanes(me ^ j if parts > 1 else 0, rows), :]
    q3[...] = split(ordered[...], 3)
    total[...] = jnp.zeros_like(total)
    copies[6].wait()
    kept, block = resid.shape[:2]
    for k in range(kept):
        total[:, lanes(ids[0, k], block)] += dot(ordered[...], resid[k], NT, HIGHEST)
        high = resid[k].astype(BF16)
        r2[0, k * block:(k + 1) * block, :] = high
        r2[1, k * block:(k + 1) * block, :] = (resid[k] - high.astype(F32)).astype(BF16)
    for copy in copies[7:]:
        copy.wait()


def next_kernel(n_x, choices, first_row, ready, *refs):
    pieces, (w, weighted, q3, before, _, _, bx, g, *outs) = refs[:n_x], refs[n_x:]
    count = ready + len(choices) * pieces[0].shape[0]
    top = bx.shape[0] - g.shape[0] + first_row
    x = bx.at[top:top + count, :]
    here = slice(first_row, first_row + count)
    pick(pieces, choices, bx.at[top + ready:top + count, :])
    tangent = jnp.tanh(jnp.dot(x[...], w[...], preferred_element_type=F32))
    grad = (weighted[here, :] * (1.0 - tangent * tangent)).astype(BF16)
    g[here, :] = grad
    yt = split(fold(dot(q3[...], grad, NT), 3), 3)
    rows, wide = outs[0].shape[0], 1024
    for i in range(bx.shape[1] // wide):
        at = slice(i * wide, (i + 1) * wide)
        total = before[:, at] + fold(dot(yt, x[:, at], NN), 3)
        for j, out in enumerate(outs):
            out[:, at] = total[j * rows:(j + 1) * rows]


def merged_kernel(ids, bx, g, resid, out):
    block = resid.shape[1]
    for k in range(ids.shape[1]):
        out[k] = dot(bx[bx.shape[0] - g.shape[0]:, lanes(ids[0, k], block)], g[...], TN) + resid[k]


def second_kernel(n_p, ids, *refs):
    parts, refs = refs[:n_p], refs[n_p:]
    g, r2, _, bx, gram = refs[:5]
    uts, pk = refs[5:-1], refs[-1]
    rank, me = pk.shape[0] // 2, lax.axis_index("dp")
    if n_p == 1:
        bx[:2 * rank, :] = split(parts[0][...], 2)
    else:
        rows = parts[0].shape[0]
        for j in range(0, n_p, 2):
            chip = (me ^ j) // 2
            swapped = me % 2 == 1
            first, second = parts[j][...], parts[j + 1][...]
            pair = jnp.concatenate([jnp.where(swapped, second, first), jnp.where(swapped, first, second)], axis=0)
            high = pair.astype(BF16)
            bx[lanes(chip, 2 * rows), :] = high
            bx[pl.ds(pl.multiple_of(rank + chip * 2 * rows, 2 * rows), 2 * rows), :] = (pair - high.astype(F32)).astype(BF16)
    block = pk.shape[1] // ids.shape[1]
    for k in range(ids.shape[1]):
        pk[:, k * block:(k + 1) * block] = bx[:2 * rank, lanes(ids[0, k], block)]
    both = fold(dot(bx[:2 * rank, :], bx[...], NT), 2)
    gram[...] = both[:, :rank] + both[:, rank:2 * rank]
    total = fold(dot(split(both[:, 2 * rank:], 3), g[...], NN), 3)
    total = total + fold(dot(pk[...], r2[0], NN), 2) + dot(pk[:rank, :], r2[1], NN)
    if len(uts) == 1:
        uts[0][...] = total
    else:
        half = rank // 2
        low_is_mine = me % 2 == 0
        uts[0][...] = jnp.where(low_is_mine, total[:half], total[half:])
        uts[1][...] = jnp.where(low_is_mine, total[half:], total[:half])


def inverse_factor(gram):
    rank, sub = gram.shape[0], 8
    blocks = rank // sub
    eye = (lax.broadcasted_iota(jnp.int32, (rank, rank), 0) == lax.broadcasted_iota(jnp.int32, (rank, rank), 1)).astype(F32)
    whole = jnp.concatenate([gram, eye], axis=1)
    rows = [whole[b * sub:(b + 1) * sub] for b in range(blocks)]
    place = lax.broadcasted_iota(jnp.int32, (sub, 2 * rank), 0)

    def column(a, k):
        return jnp.take_along_axis(a, jnp.full(a.shape, k, jnp.int32), axis=1)

    out = []
    for b in range(blocks):
        panel = rows[b]
        entry = [column(panel, b * sub + j) for j in range(sub)]
        pivots = jnp.zeros_like(panel)
        scale = []
        for i in range(sub):
            scale.append(1.0 / entry[i][i:i + 1, :])
            pivots = jnp.where(place == i, entry[i], pivots)
            ratio = jnp.where(place > i, entry[i], 0.0) * scale[i]
            panel = panel - ratio * panel[i:i + 1, :]
            for j in range(i + 1, sub):
                entry[j] = entry[j] - ratio * entry[j][i:i + 1, :]
        out.append((panel / jnp.sqrt(pivots))[:, rank:])
        solved = [panel[i:i + 1, :] * scale[i] for i in range(sub)]
        for i in range(sub - 1, -1, -1):
            for j in range(i + 1, sub):
                solved[i] = solved[i] - (entry[j][i:i + 1, :] * scale[i]) * solved[j]
        for c in range(b + 1, blocks):
            update = column(rows[c], b * sub) * solved[0]
            for j in range(1, sub):
                update = update + column(rows[c], b * sub + j) * solved[j]
            rows[c] = rows[c] - update
    return jnp.concatenate(out, axis=0)


def factor_kernel(ids, gram, bx, pft, linv, blocks):
    rank = gram.shape[0]
    inverse = inverse_factor(gram[...])
    linv[...] = inverse
    high = inverse.astype(BF16)
    low = (inverse - high.astype(F32)).astype(BF16)
    lhs = jnp.concatenate([jnp.concatenate([high, high], axis=1), jnp.concatenate([low, jnp.zeros_like(low)], axis=1)], axis=0)
    wide = 1024
    for i in range(pft.shape[1] // wide):
        at = slice(i * wide, (i + 1) * wide)
        pft[:, at] = fold(dot(lhs, bx[:2 * rank, at], NN), 2)
    block = blocks.shape[0] // ids.shape[1]
    for k in range(ids.shape[1]):
        piece = jnp.transpose(pft[:, lanes(ids[0, k], block)])
        high = piece.astype(BF16)
        low = (piece - high.astype(F32)).astype(BF16)
        blocks[k * block:(k + 1) * block, :] = jnp.concatenate([high, low, high], axis=1)


def last_kernel(n_u, scale, *refs):
    halves, (linv, blocks, merged, qt, out, ut, made, sent) = refs[:n_u], refs[n_u:]
    if n_u == 1:
        ut[...] = halves[0][...]
    else:
        rows, core = halves[0].shape[0], lax.axis_index("dp") % 2
        ut[lanes(core, rows), :] = halves[0][...]
        ut[lanes(1 - core, rows), :] = halves[1][...]
    q = dot(linv[...], ut[...], NN, HIGHEST) * scale
    qt[...] = q
    two = split(q, 2)
    rank = q.shape[0]
    rhs = jnp.concatenate([two[:rank], two[:rank], two[rank:]], axis=0)
    block = merged.shape[1]
    copies = []
    for k in range(merged.shape[0]):
        made[k] = merged[k] - dot(blocks[k * block:(k + 1) * block, :], rhs, NN)
        copies.append(pltpu.make_async_copy(made.at[k], out.at[k], sent.at[k]))
        copies[-1].start()
    for copy in copies:
        copy.wait()


def gather_rows(x, groups, prepared, first_stage):
    if groups != 4:
        rows = x.shape[0]
        whole = lax.all_gather(x, "mp", axis=0, tiled=True)
        pieces = [whole[j * rows:(j + 1) * rows] for j in range(groups)]
        done = first_stage(pieces[:-2], [(j, None) for j in range(groups - 2)], 0)
        return done, [(pieces[j:j + 1], [(0, None)]) for j in (groups - 2, groups - 1)]
    outer = [(0, 1), (1, 0), (2, 3), (3, 2)]
    inner = [(1, 2), (2, 1)]
    a0 = lax.ppermute(x, "mp", outer)
    b0 = lax.ppermute(together(x, lax.axis_index("mp") * 2)[0], "mp", inner)
    a0, _ = together(a0, prepared)
    b1 = lax.ppermute(a0, "mp", inner)
    a1 = lax.ppermute(b0, "mp", outer)
    done = first_stage([a0], [(0, None)], x.shape[0])
    b1, *done = together(b1, *done)
    a2 = lax.ppermute(b1, "mp", outer)
    return done, [([a1, b0], [(0, 1)]), ([a2, b1], [(0, 1)])]


def swap(a, bit, size):
    return lax.ppermute(a, "dp", [(i, i ^ bit) for i in range(size)])


def together(*values):
    return lax.optimization_barrier(values)


def shards(gen_rows, lengths, assign, rewards, upstream, weight, q_init, resid, block_ids):
    groups, replicas = lax.axis_size("mp"), lax.axis_size("dp")
    slot_count, depth = gen_rows.shape
    columns, rank = q_init.shape
    kept, block = resid.shape[:2]
    rows = groups * slot_count
    ids = block_ids.reshape(1, kept)
    direct = replicas == 8
    shape = jax.ShapeDtypeStruct
    wide_rows, grad_rows = shape((2 * rank + rows, depth), BF16), shape((rows, columns), BF16)

    far = (lengths, assign, rewards, ids, upstream, q_init.T, resid, weight, gen_rows)
    far = [pltpu.with_memory_space_constraint(a, pltpu.HBM) for a in far]
    ids, weight, resid, bx, weighted, q3, r2, pt = call(
        functools.partial(prepare_kernel, replicas if direct else 1, groups == 4),
        [shape(ids.shape, jnp.int32), shape(weight.shape, BF16), shape(resid.shape, F32), wide_rows,
         shape((rows, columns), F32), shape((3 * rank, columns), BF16), shape((2, kept * block, columns), BF16),
         shape((rank, depth), F32)],
        [pltpu.VMEM((rank, columns), F32), pltpu.VMEM(upstream.shape, BF16), pltpu.VMEM((rank, columns), F32),
         pltpu.VMEM(lengths.shape, jnp.int32), pltpu.VMEM(assign.shape, jnp.int32), pltpu.VMEM(rewards.shape, F32),
         pltpu.SemaphoreType.DMA((9,))], name="prepare", far=len(far), grant=PREPARE_GRANT,
    )(*far)

    def stage(pieces, choices, first_row, ready, bx, g, pt, outs):
        n = len(pieces)
        return call(
            functools.partial(next_kernel, n, choices, first_row, ready), [wide_rows, grad_rows] + outs,
            flops=2 * slot_count * depth * columns, name="rows", aliases={n + 4: 0, n + 5: 1},
        )(*pieces, weight, weighted, q3, pt, bx, g)

    whole_rank = [shape((rank, depth), F32)]
    (bx, g, pt), stages = gather_rows(
        gen_rows, groups, weighted,
        lambda pieces, choices, ready: stage(pieces, choices, 0, ready, bx, jnp.zeros(grad_rows.shape, BF16), pt, whole_rank),
    )
    for i, (pieces, choices) in enumerate(stages):
        last = i == len(stages) - 1
        outs = [shape((rank // replicas, depth), F32)] * replicas if last and direct else whole_rank
        bx, g, *parts = stage(pieces, choices, rows - (len(stages) - i) * slot_count, 0, bx, g, pt, outs)
        pt = parts[0]

    merged = call(merged_kernel, shape((kept, block, columns), F32), name="merged")(ids, bx, g, resid)

    if direct:
        chips = replicas // 2
        sums = [parts[2 * k] + swap(parts[2 * k + 1], 1, replicas) for k in range(chips)]
        got = [swap(sums[k], 2 * k, replicas) for k in range(1, chips)]
        *got, merged = together(*got, merged)
        own = sums[0] + got[0] + got[1] + got[2]
        same = [own] + [swap(own, 2 * k, replicas) for k in range(1, chips)]
        p_parts = []
        for s in same:
            p_parts += [s, swap(s, 1, replicas)]
        u_shapes = [shape((rank // 2, columns), F32)] * 2
    else:
        p_parts = [lax.psum(parts[0], "dp")]
        u_shapes = [shape((rank, columns), F32)]

    n_p = len(p_parts)
    bx, gram, *us = call(
        functools.partial(second_kernel, n_p),
        [wide_rows, shape((rank, rank), F32)] + u_shapes,
        [pltpu.VMEM((2 * rank, kept * block), BF16)], name="second", aliases={n_p + 3: 0},
    )(ids, *p_parts, g, r2, bx)

    pft, linv, blocks = call(
        factor_kernel,
        [shape((rank, depth), F32), shape((rank, rank), F32), shape((kept * block, 3 * rank), BF16)], name="factor",
    )(ids, gram, bx)

    if direct:
        chip_sum = us[0] + swap(us[1], 1, replicas)
        got = [swap(chip_sum, 2 * k, replicas) for k in range(1, chips)]
        *got, linv = together(*got, linv)
        total = chip_sum + got[0] + got[1] + got[2]
        u_parts = [total, swap(total, 1, replicas)]
    else:
        u_parts = [lax.psum(us[0], "dp")]
    n_u = len(u_parts)
    qt, new_resid = call(
        functools.partial(last_kernel, n_u, 1.0 / replicas),
        [shape((rank, columns), F32), shape((kept, block, columns), F32)],
        [pltpu.VMEM((rank, columns), F32), pltpu.VMEM((kept, block, columns), F32), pltpu.SemaphoreType.DMA((kept,))],
        name="last", out_specs=[VMEM, pl.BlockSpec(memory_space=pl.ANY)],
    )(*u_parts, linv, blocks, merged)
    return pft.T, qt.T, new_resid


def solution(mesh):
    placed = (
        P(("dp", "mp"), None),
        P("dp", None),
        P("dp", None),
        P("dp", None),
        P("dp", "mp"),
        P(None, "mp"),
        P("mp", None),
        P("dp", None, "mp"),
        P("dp"),
    )
    return jax.shard_map(
        shards,
        mesh=mesh,
        in_specs=placed,
        out_specs=(P(None, "mp"), P("mp", None), P("dp", None, "mp")),
        check_vma=False,
    )
```

```python
import functools
import jax
import jax.numpy as jnp
from jax import lax
from jax.experimental import pallas as pl
from jax.experimental.pallas import tpu as pltpu
from jax.sharding import PartitionSpec as P

F32 = jnp.float32
BF16 = jnp.bfloat16
HIGHEST = lax.Precision.HIGHEST
VMEM_LIMIT = 16 * 1024 * 1024
PREPARE_GRANT = 40 * 1024 * 1024


def dot(a, b, dims, precision=None):
    return lax.dot_general(a, b, (dims, ((), ())), precision=precision, preferred_element_type=F32)


NN, NT, TN = ((1,), (0,)), ((1,), (1,)), ((0,), (0,))
VMEM = pl.BlockSpec(memory_space=pltpu.VMEM)
HBM = pl.BlockSpec(memory_space=pltpu.HBM)


def split(a, parts):
    out = []
    for _ in range(parts):
        high = a.astype(BF16)
        out.append(high)
        a = a - high.astype(F32)
    return jnp.concatenate(out, axis=0)


def fold(a, parts):
    rows = a.shape[0] // parts
    total = a[:rows]
    for i in range(1, parts):
        total = total + a[i * rows:(i + 1) * rows]
    return total


def lanes(index, width):
    return pl.ds(pl.multiple_of(index * width, width), width)


def call(kernel, outs, scratch=(), flops=1000000, name=None, aliases=None, out_specs=None, far=0, grant=VMEM_LIMIT):
    def run(*args):
        return pl.pallas_call(
            kernel,
            input_output_aliases=aliases or {},
            out_shape=outs,
            in_specs=[HBM] * far + [VMEM] * (len(args) - far),
            out_specs=out_specs or jax.tree.map(lambda _: VMEM, outs),
            scratch_shapes=list(scratch),
            compiler_params=pltpu.CompilerParams(vmem_limit_bytes=grant),
            cost_estimate=pl.CostEstimate(flops=flops, bytes_accessed=1000000, transcendentals=0),
            name=name,
        )(*args)

    return run


def pick(pieces, choices, out):
    rows = out.shape[0] // len(choices)
    for j, (first, second) in enumerate(choices):
        here = slice(j * rows, (j + 1) * rows)
        if second is None:
            out[here, :] = pieces[first][...]
        else:
            at = lax.axis_index("mp")
            at_end = (at == 0) | (at == lax.axis_size("mp") - 1)

            @pl.when(at_end)
            def _():
                out[here, :] = pieces[first][...]

            @pl.when(jnp.logical_not(at_end))
            def _():
                out[here, :] = pieces[second][...]


def begin_kernel(w, end, between, _, bx, hidden):
    cut = end.shape[1]
    x = bx.at[bx.shape[0] - end.shape[0]:, :cut]
    pick([end, between.at[:, :cut]], [(0, 1)], x)
    hidden[...] = jnp.dot(x[...], w[:cut, :], preferred_element_type=F32)


def weigh_rows(lengths, assign, rewards, upstream, order, weighted):
    groups, sequences = lengths.shape
    slots = upstream.shape[0]
    capacity = slots // (groups * groups)
    count = weighted.shape[0] // groups
    row = lax.broadcasted_iota(jnp.int32, (count, slots), 0)
    slot = lax.broadcasted_iota(jnp.int32, (count, slots), 1)
    row_only = lax.broadcasted_iota(jnp.int32, (count, 1), 0)
    for j, source in enumerate(order):
        picked = jnp.zeros((count, slots), jnp.bool_)
        gain, size = jnp.zeros((count, 1), F32), jnp.ones((count, 1), F32)
        total = rewards[source, 0]
        for s in range(1, sequences):
            total = total + rewards[source, s]
        mean = total * (1.0 / sequences)
        offset = jnp.int32(0)
        for s in range(sequences):
            length = lengths[source, s]
            base = assign[source, s] * (groups * capacity) + source * capacity - offset
            inside = (row >= offset) & (row < offset + length)
            picked = picked | (inside & (slot == row + base))
            inside = (row_only >= offset) & (row_only < offset + length)
            gain = jnp.where(inside, rewards[source, s] - mean, gain)
            size = jnp.where(inside, length.astype(F32), size)
            offset = offset + length
        rows = jnp.dot(picked.astype(F32).astype(BF16), upstream[...], preferred_element_type=F32)
        weighted[j * count:(j + 1) * count, :] = gain / size * rows


def gather_order(groups):
    if groups != 4:
        return list(range(groups))
    at = lax.axis_index("mp")
    low = at < 2
    return [at, at ^ 1, jnp.where(low, 2, 1), jnp.where(low, 3, 0)]


def prepare_kernel(parts, own, *refs):
    small, (upstream_far, q0t_far, resid_far, w, x), refs = refs[:4], refs[4:9], refs[9:]
    ids, w_near, resid, bx, weighted, q3, r2, total, ordered, upstream, q0t, lengths, assign, rewards, arrived = refs
    pairs = list(zip(small, (lengths, assign, rewards, ids)))
    pairs += [(upstream_far, upstream), (q0t_far, q0t), (resid_far, resid), (w, w_near)]
    if own:
        first = bx.shape[0] - weighted.shape[0]
        pairs.append((x, bx.at[first:first + x.shape[0], :]))
    copies = [pltpu.make_async_copy(a, b, arrived.at[i]) for i, (a, b) in enumerate(pairs)]
    for copy in copies:
        copy.start()
    for copy in copies[:5]:
        copy.wait()
    weigh_rows(lengths, assign, rewards, upstream, gather_order(lengths.shape[0]), weighted)
    copies[5].wait()
    rows, me = ordered.shape[0] // parts, lax.axis_index("dp")
    for j in range(parts):
        ordered[j * rows:(j + 1) * rows, :] = q0t[lanes(me ^ j if parts > 1 else 0, rows), :]
    q3[...] = split(ordered[...], 3)
    total[...] = jnp.zeros_like(total)
    copies[6].wait()
    kept, block = resid.shape[:2]
    for k in range(kept):
        total[:, lanes(ids[0, k], block)] += dot(ordered[...], resid[k], NT, HIGHEST)
        high = resid[k].astype(BF16)
        r2[0, k * block:(k + 1) * block, :] = high
        r2[1, k * block:(k + 1) * block, :] = (resid[k] - high.astype(F32)).astype(BF16)
    for copy in copies[7:]:
        copy.wait()


def next_kernel(n_x, choices, first_row, ready, cut, *refs):
    pieces, (w, weighted, q3, before, *refs) = refs[:n_x], refs[n_x:]
    (begun,), refs = (refs[:1], refs[1:]) if cut else ((None,), refs)
    _, _, bx, g, *outs = refs
    count = ready + len(choices) * pieces[0].shape[0]
    top = bx.shape[0] - g.shape[0] + first_row
    x = bx.at[top:top + count, :]
    here = slice(first_row, first_row + count)
    if cut:
        pick([pieces[0], pieces[1].at[:, cut:]], choices, bx.at[top + ready:top + count, cut:])
    else:
        pick(pieces, choices, bx.at[top + ready:top + count, :])
    hidden = jnp.dot(x[:, cut:], w[cut:, :], preferred_element_type=F32)
    if cut:
        hidden = begun[...] + hidden
    tangent = jnp.tanh(hidden)
    grad = (weighted[here, :] * (1.0 - tangent * tangent)).astype(BF16)
    g[here, :] = grad
    yt = split(fold(dot(q3[...], grad, NT), 3), 3)
    rows, wide = outs[0].shape[0], 1024
    for i in range(bx.shape[1] // wide):
        at = slice(i * wide, (i + 1) * wide)
        total = before[:, at] + fold(dot(yt, x[:, at], NN), 3)
        for j, out in enumerate(outs):
            out[:, at] = total[j * rows:(j + 1) * rows]


def merged_kernel(ids, bx, g, resid, out):
    block = resid.shape[1]
    for k in range(ids.shape[1]):
        out[k] = dot(bx[bx.shape[0] - g.shape[0]:, lanes(ids[0, k], block)], g[...], TN) + resid[k]


def second_kernel(n_p, ids, *refs):
    parts, refs = refs[:n_p], refs[n_p:]
    g, r2, _, bx, gram = refs[:5]
    uts, pk = refs[5:-1], refs[-1]
    rank, me = pk.shape[0] // 2, lax.axis_index("dp")
    if n_p == 1:
        bx[:2 * rank, :] = split(parts[0][...], 2)
    else:
        rows = parts[0].shape[0]
        for j in range(0, n_p, 2):
            chip = (me ^ j) // 2
            swapped = me % 2 == 1
            first, second = parts[j][...], parts[j + 1][...]
            pair = jnp.concatenate([jnp.where(swapped, second, first), jnp.where(swapped, first, second)], axis=0)
            high = pair.astype(BF16)
            bx[lanes(chip, 2 * rows), :] = high
            bx[pl.ds(pl.multiple_of(rank + chip * 2 * rows, 2 * rows), 2 * rows), :] = (pair - high.astype(F32)).astype(BF16)
    block = pk.shape[1] // ids.shape[1]
    for k in range(ids.shape[1]):
        pk[:, k * block:(k + 1) * block] = bx[:2 * rank, lanes(ids[0, k], block)]
    both = dot(bx[...], bx[:2 * rank, :], NT)
    both = both[:, :rank] + both[:, rank:]
    gram[...] = fold(both[:2 * rank], 2)
    total = fold(dot(split(jnp.transpose(both[2 * rank:]), 3), g[...], NN), 3)
    total = total + fold(dot(pk[...], r2[0], NN), 2) + dot(pk[:rank, :], r2[1], NN)
    if len(uts) == 1:
        uts[0][...] = total
    else:
        half = rank // 2
        low_is_mine = me % 2 == 0
        uts[0][...] = jnp.where(low_is_mine, total[:half], total[half:])
        uts[1][...] = jnp.where(low_is_mine, total[half:], total[:half])


def inverse_factor(gram):
    rank, sub = gram.shape[0], 8
    blocks = rank // sub
    eye = (lax.broadcasted_iota(jnp.int32, (rank, rank), 0) == lax.broadcasted_iota(jnp.int32, (rank, rank), 1)).astype(F32)
    whole = jnp.concatenate([gram, eye], axis=1)
    rows = [whole[b * sub:(b + 1) * sub] for b in range(blocks)]
    place = lax.broadcasted_iota(jnp.int32, (sub, 2 * rank), 0)

    def column(a, k):
        return jnp.take_along_axis(a, jnp.full(a.shape, k, jnp.int32), axis=1)

    out = []
    for b in range(blocks):
        panel = rows[b]
        entry = [column(panel, b * sub + j) for j in range(sub)]
        pivots = jnp.zeros_like(panel)
        scale = []
        for i in range(sub):
            scale.append(1.0 / entry[i][i:i + 1, :])
            pivots = jnp.where(place == i, entry[i], pivots)
            ratio = jnp.where(place > i, entry[i], 0.0) * scale[i]
            panel = panel - ratio * panel[i:i + 1, :]
            for j in range(i + 1, sub):
                entry[j] = entry[j] - ratio * entry[j][i:i + 1, :]
        out.append((panel / jnp.sqrt(pivots))[:, rank:])
        solved = [panel[i:i + 1, :] * scale[i] for i in range(sub)]
        for i in range(sub - 1, -1, -1):
            for j in range(i + 1, sub):
                solved[i] = solved[i] - (entry[j][i:i + 1, :] * scale[i]) * solved[j]
        for c in range(b + 1, blocks):
            update = column(rows[c], b * sub) * solved[0]
            for j in range(1, sub):
                update = update + column(rows[c], b * sub + j) * solved[j]
            rows[c] = rows[c] - update
    return jnp.concatenate(out, axis=0)


def factor_kernel(gram, linv):
    linv[...] = inverse_factor(gram[...])


def left_kernel(ids, linv, bx, pft, blocks):
    rank = linv.shape[0]
    high = linv[...].astype(BF16)
    low = (linv[...] - high.astype(F32)).astype(BF16)
    lhs = jnp.concatenate([jnp.concatenate([high, high], axis=1), jnp.concatenate([low, jnp.zeros_like(low)], axis=1)], axis=0)
    wide = 1024
    for i in range(pft.shape[1] // wide):
        at = slice(i * wide, (i + 1) * wide)
        pft[:, at] = fold(dot(lhs, bx[:2 * rank, at], NN), 2)
    block = blocks.shape[0] // ids.shape[1]
    for k in range(ids.shape[1]):
        piece = jnp.transpose(pft[:, lanes(ids[0, k], block)])
        high = piece.astype(BF16)
        low = (piece - high.astype(F32)).astype(BF16)
        blocks[k * block:(k + 1) * block, :] = jnp.concatenate([high, low, high], axis=1)


def last_kernel(n_u, scale, *refs):
    halves, (linv, blocks, merged, qt, out, ut, right, made, sent) = refs[:n_u], refs[n_u:]
    if n_u == 1:
        ut[...] = halves[0][...]
    else:
        rows, core = halves[0].shape[0], lax.axis_index("dp") % 2
        ut[lanes(core, rows), :] = halves[0][...]
        ut[lanes(1 - core, rows), :] = halves[1][...]
    q = dot(linv[...], ut[...], NN, HIGHEST) * scale
    right[...] = q
    copies = [pltpu.make_async_copy(right, qt, sent.at[merged.shape[0]])]
    copies[0].start()
    two = split(q, 2)
    rank = q.shape[0]
    rhs = jnp.concatenate([two[:rank], two[:rank], two[rank:]], axis=0)
    block = merged.shape[1]
    for k in range(merged.shape[0]):
        made[k] = merged[k] - dot(blocks[k * block:(k + 1) * block, :], rhs, NN)
        copies.append(pltpu.make_async_copy(made.at[k], out.at[k], sent.at[k]))
        copies[-1].start()
    for copy in copies:
        copy.wait()


def gather_rows(x, groups, prepared, first_stage):
    if groups != 4:
        rows = x.shape[0]
        whole = lax.all_gather(x, "mp", axis=0, tiled=True)
        pieces = [whole[j * rows:(j + 1) * rows] for j in range(groups)]
        done = first_stage(pieces[:-2], [(j, None) for j in range(groups - 2)], 0)
        return done, [(pieces[j:j + 1], [(0, None)]) for j in (groups - 2, groups - 1)]
    outer = [(0, 1), (1, 0), (2, 3), (3, 2)]
    inner = [(1, 2), (2, 1)]
    a0 = lax.ppermute(x, "mp", outer)
    b0 = lax.ppermute(together(x, lax.axis_index("mp") * 2)[0], "mp", inner)
    a0, _ = together(a0, prepared)
    b1 = lax.ppermute(a0, "mp", inner)
    a1 = lax.ppermute(b0, "mp", outer)
    done = first_stage([a0], [(0, None)], x.shape[0])
    b1, *done = together(b1, *done)
    cut = x.shape[1] * 3 // 4
    a2 = [lax.ppermute(part, "mp", outer) for part in (b1[:, :cut], b1[:, cut:])]
    return done, [([a1, b0], [(0, 1)]), ([a2[0], b1], [(0, 1)]), ([a2[1], b1], [(0, 1)])]


def swap(a, bit, size):
    return lax.ppermute(a, "dp", [(i, i ^ bit) for i in range(size)])


def together(*values):
    return lax.optimization_barrier(values)


def shards(gen_rows, lengths, assign, rewards, upstream, weight, q_init, resid, block_ids):
    groups, replicas = lax.axis_size("mp"), lax.axis_size("dp")
    slot_count, depth = gen_rows.shape
    columns, rank = q_init.shape
    kept, block = resid.shape[:2]
    rows = groups * slot_count
    ids = block_ids.reshape(1, kept)
    direct = replicas == 8
    shape = jax.ShapeDtypeStruct
    wide_rows, grad_rows = shape((2 * rank + rows, depth), BF16), shape((rows, columns), BF16)

    far = (lengths, assign, rewards, ids, upstream, q_init.T, resid, weight, gen_rows)
    far = [pltpu.with_memory_space_constraint(a, pltpu.HBM) for a in far]
    ids, weight, resid, bx, weighted, q3, r2, pt = call(
        functools.partial(prepare_kernel, replicas if direct else 1, groups == 4),
        [shape(ids.shape, jnp.int32), shape(weight.shape, BF16), shape(resid.shape, F32), wide_rows,
         shape((rows, columns), F32), shape((3 * rank, columns), BF16), shape((2, kept * block, columns), BF16),
         shape((rank, depth), F32)],
        [pltpu.VMEM((rank, columns), F32), pltpu.VMEM(upstream.shape, BF16), pltpu.VMEM((rank, columns), F32),
         pltpu.VMEM(lengths.shape, jnp.int32), pltpu.VMEM(assign.shape, jnp.int32), pltpu.VMEM(rewards.shape, F32),
         pltpu.SemaphoreType.DMA((9,))], name="prepare", far=len(far), grant=PREPARE_GRANT,
    )(*far)

    def stage(pieces, choices, first_row, ready, bx, g, pt, outs, begun=()):
        n = len(pieces)
        cut = depth - pieces[0].shape[1]
        return call(
            functools.partial(next_kernel, n, choices, first_row, ready, cut), [wide_rows, grad_rows] + outs,
            flops=2 * slot_count * depth * columns, name="rows", aliases={n + 4 + len(begun): 0, n + 5 + len(begun): 1},
        )(*pieces, weight, weighted, q3, pt, *begun, bx, g)

    whole_rank = [shape((rank, depth), F32)]
    (bx, g, pt), stages = gather_rows(
        gen_rows, groups, weighted,
        lambda pieces, choices, ready: stage(pieces, choices, 0, ready, bx, jnp.zeros(grad_rows.shape, BF16), pt, whole_rank),
    )
    final = [shape((rank // replicas, depth), F32)] * replicas if direct else whole_rank
    bx, g, pt = stage(*stages[0], rows - 2 * slot_count, 0, bx, g, pt, whole_rank)
    begun = ()
    if len(stages) == 3:
        bx, *begun = call(
            begin_kernel, [wide_rows, shape((slot_count, columns), F32)], name="begin", aliases={3: 0},
        )(weight, *stages[1][0], bx)
    bx, g, *parts = stage(*stages[-1], rows - slot_count, 0, bx, g, pt, final, begun)

    merged = call(merged_kernel, shape((kept, block, columns), F32), name="merged")(ids, bx, g, resid)

    if direct:
        chips = replicas // 2
        sums = [parts[2 * k] + swap(parts[2 * k + 1], 1, replicas) for k in range(chips)]
        got = [swap(sums[k], 2 * k, replicas) for k in range(1, chips)]
        *got, merged = together(*got, merged)
        own = sums[0] + got[0] + got[1] + got[2]
        same = [own] + [swap(own, 2 * k, replicas) for k in range(1, chips)]
        p_parts = []
        for s in same:
            p_parts += [s, swap(s, 1, replicas)]
        u_shapes = [shape((rank // 2, columns), F32)] * 2
    else:
        p_parts = [lax.psum(parts[0], "dp")]
        u_shapes = [shape((rank, columns), F32)]

    n_p = len(p_parts)
    bx, gram, *us = call(
        functools.partial(second_kernel, n_p),
        [wide_rows, shape((rank, rank), F32)] + u_shapes,
        [pltpu.VMEM((2 * rank, kept * block), BF16)], name="second", aliases={n_p + 3: 0},
    )(ids, *p_parts, g, r2, bx)

    linv = call(factor_kernel, shape((rank, rank), F32), name="factor")(gram)

    if direct:
        chip_sum = us[0] + swap(us[1], 1, replicas)
        got = [swap(chip_sum, 2 * k, replicas) for k in range(1, chips)]
        *got, linv = together(*got, linv)
        total = chip_sum + got[0] + got[1] + got[2]
        bx, total = together(bx, total)
        u_parts = [total, swap(total, 1, replicas)]
    else:
        u_parts = [lax.psum(us[0], "dp")]
    pft, blocks = call(
        left_kernel, [shape((rank, depth), F32), shape((kept * block, 3 * rank), BF16)], name="left",
    )(ids, linv, bx)
    if direct:
        other, blocks = together(u_parts[1], blocks)
        u_parts = [u_parts[0], other]
    n_u = len(u_parts)
    qt, new_resid = call(
        functools.partial(last_kernel, n_u, 1.0 / replicas),
        [shape((rank, columns), F32), shape((kept, block, columns), F32)],
        [pltpu.VMEM((rank, columns), F32), pltpu.VMEM((rank, columns), F32),
         pltpu.VMEM((kept, block, columns), F32), pltpu.SemaphoreType.DMA((kept + 1,))],
        name="last", out_specs=[pl.BlockSpec(memory_space=pl.ANY)] * 2,
    )(*u_parts, linv, blocks, merged)
    return pft.T, qt.T, new_resid


def solution(mesh):
    placed = (
        P(("dp", "mp"), None),
        P("dp", None),
        P("dp", None),
        P("dp", None),
        P("dp", "mp"),
        P(None, "mp"),
        P("mp", None),
        P("dp", None, "mp"),
        P("dp"),
    )
    return jax.shard_map(
        shards,
        mesh=mesh,
        in_specs=placed,
        out_specs=(P(None, "mp"), P("mp", None), P("dp", None, "mp")),
        check_vma=False,
    )
```

```python
import functools
import jax
import jax.numpy as jnp
from jax import lax
from jax.experimental import pallas as pl
from jax.experimental.pallas import tpu as pltpu
from jax.sharding import PartitionSpec as P

F32 = jnp.float32
BF16 = jnp.bfloat16
HIGHEST = lax.Precision.HIGHEST
VMEM_LIMIT = 16 * 1024 * 1024
PREPARE_GRANT = 40 * 1024 * 1024


def dot(a, b, dims, precision=None):
    return lax.dot_general(a, b, (dims, ((), ())), precision=precision, preferred_element_type=F32)


NN, NT, TN = ((1,), (0,)), ((1,), (1,)), ((0,), (0,))
VMEM = pl.BlockSpec(memory_space=pltpu.VMEM)
HBM = pl.BlockSpec(memory_space=pltpu.HBM)


def split(a, parts, axis=0):
    out = []
    for _ in range(parts):
        high = a.astype(BF16)
        out.append(high)
        a = a - high.astype(F32)
    return jnp.concatenate(out, axis=axis)


def fold(a, parts):
    rows = a.shape[0] // parts
    total = a[:rows]
    for i in range(1, parts):
        total = total + a[i * rows:(i + 1) * rows]
    return total


def lanes(index, width):
    return pl.ds(pl.multiple_of(index * width, width), width)


def call(kernel, outs, scratch=(), flops=1000000, name=None, aliases=None, out_specs=None, far=0, grant=VMEM_LIMIT):
    def run(*args):
        return pl.pallas_call(
            kernel,
            input_output_aliases=aliases or {},
            out_shape=outs,
            in_specs=[HBM] * far + [VMEM] * (len(args) - far),
            out_specs=out_specs or jax.tree.map(lambda _: VMEM, outs),
            scratch_shapes=list(scratch),
            compiler_params=pltpu.CompilerParams(vmem_limit_bytes=grant),
            cost_estimate=pl.CostEstimate(flops=flops, bytes_accessed=1000000, transcendentals=0),
            name=name,
        )(*args)

    return run


def pick(pieces, choices, out):
    rows = out.shape[0] // len(choices)
    for j, (first, second) in enumerate(choices):
        here = slice(j * rows, (j + 1) * rows)
        if second is None:
            out[here, :] = pieces[first][...]
        else:
            at = lax.axis_index("mp")
            at_end = (at == 0) | (at == lax.axis_size("mp") - 1)

            @pl.when(at_end)
            def _():
                out[here, :] = pieces[first][...]

            @pl.when(jnp.logical_not(at_end))
            def _():
                out[here, :] = pieces[second][...]


def begin_kernel(w, end, between, _, bx, hidden):
    cut = end.shape[1]
    x = bx.at[bx.shape[0] - end.shape[0]:, :cut]
    pick([end, between.at[:, :cut]], [(0, 1)], x)
    hidden[...] = jnp.dot(x[...], w[:cut, :], preferred_element_type=F32)


def weigh_rows(lengths, assign, rewards, upstream, order, weighted):
    groups, sequences = lengths.shape
    slots = upstream.shape[0]
    capacity = slots // (groups * groups)
    count = weighted.shape[0] // groups
    row = lax.broadcasted_iota(jnp.int32, (count, slots), 0)
    slot = lax.broadcasted_iota(jnp.int32, (count, slots), 1)
    row_only = lax.broadcasted_iota(jnp.int32, (count, 1), 0)
    for j, source in enumerate(order):
        picked = jnp.zeros((count, slots), jnp.bool_)
        gain, size = jnp.zeros((count, 1), F32), jnp.ones((count, 1), F32)
        total = rewards[source, 0]
        for s in range(1, sequences):
            total = total + rewards[source, s]
        mean = total * (1.0 / sequences)
        offset = jnp.int32(0)
        for s in range(sequences):
            length = lengths[source, s]
            base = assign[source, s] * (groups * capacity) + source * capacity - offset
            inside = (row >= offset) & (row < offset + length)
            picked = picked | (inside & (slot == row + base))
            inside = (row_only >= offset) & (row_only < offset + length)
            gain = jnp.where(inside, rewards[source, s] - mean, gain)
            size = jnp.where(inside, length.astype(F32), size)
            offset = offset + length
        rows = jnp.dot(picked.astype(F32).astype(BF16), upstream[...], preferred_element_type=F32)
        weighted[j * count:(j + 1) * count, :] = gain / size * rows


def gather_order(groups):
    if groups != 4:
        return list(range(groups))
    at = lax.axis_index("mp")
    low = at < 2
    return [at, at ^ 1, jnp.where(low, 2, 1), jnp.where(low, 3, 0)]


def prepare_kernel(parts, own, *refs):
    small, (upstream_far, q0t_far, resid_far, w, x), refs = refs[:4], refs[4:9], refs[9:]
    ids, w_near, resid, bx, weighted, q3, r2, total, ordered, upstream, q0t, lengths, assign, rewards, arrived = refs
    pairs = list(zip(small, (lengths, assign, rewards, ids)))
    pairs += [(upstream_far, upstream), (q0t_far, q0t), (resid_far, resid), (w, w_near)]
    if own:
        first = bx.shape[0] - weighted.shape[0]
        pairs.append((x, bx.at[first:first + x.shape[0], :]))
    copies = [pltpu.make_async_copy(a, b, arrived.at[i]) for i, (a, b) in enumerate(pairs)]
    for copy in copies:
        copy.start()
    for copy in copies[:5]:
        copy.wait()
    weigh_rows(lengths, assign, rewards, upstream, gather_order(lengths.shape[0]), weighted)
    copies[5].wait()
    rows, me = ordered.shape[0] // parts, lax.axis_index("dp")
    for j in range(parts):
        ordered[j * rows:(j + 1) * rows, :] = q0t[lanes(me ^ j if parts > 1 else 0, rows), :]
    q3[...] = split(ordered[...], 3)
    total[...] = jnp.zeros_like(total)
    copies[6].wait()
    kept, block = resid.shape[:2]
    for k in range(kept):
        total[:, lanes(ids[0, k], block)] += dot(ordered[...], resid[k], NT, HIGHEST)
        high = resid[k].astype(BF16)
        r2[0, k * block:(k + 1) * block, :] = high
        r2[1, k * block:(k + 1) * block, :] = (resid[k] - high.astype(F32)).astype(BF16)
    for copy in copies[7:]:
        copy.wait()


def next_kernel(n_x, choices, first_row, ready, cut, *refs):
    pieces, (w, weighted, q3, before, *refs) = refs[:n_x], refs[n_x:]
    (begun,), refs = (refs[:1], refs[1:]) if cut else ((None,), refs)
    _, _, bx, g, *outs = refs
    count = ready + len(choices) * pieces[0].shape[0]
    top = bx.shape[0] - g.shape[0] + first_row
    x = bx.at[top:top + count, :]
    here = slice(first_row, first_row + count)
    if cut:
        pick([pieces[0], pieces[1].at[:, cut:]], choices, bx.at[top + ready:top + count, cut:])
    else:
        pick(pieces, choices, bx.at[top + ready:top + count, :])
    hidden = jnp.dot(x[:, cut:], w[cut:, :], preferred_element_type=F32)
    if cut:
        hidden = begun[...] + hidden
    tangent = jnp.tanh(hidden)
    grad = (weighted[here, :] * (1.0 - tangent * tangent)).astype(BF16)
    g[here, :] = grad
    yt = split(fold(dot(q3[...], grad, NT), 3), 3, axis=1)
    rows, wide = outs[0].shape[0], 1024
    for i in range(bx.shape[1] // wide):
        at = slice(i * wide, (i + 1) * wide)
        total = before[:, at] + dot(yt, jnp.concatenate([x[:, at]] * 3, axis=0), NN)
        for j, out in enumerate(outs):
            out[:, at] = total[j * rows:(j + 1) * rows]


def merged_kernel(ids, bx, g, resid, out):
    block = resid.shape[1]
    for k in range(ids.shape[1]):
        out[k] = dot(bx[bx.shape[0] - g.shape[0]:, lanes(ids[0, k], block)], g[...], TN) + resid[k]


def second_kernel(n_p, ids, *refs):
    parts, refs = refs[:n_p], refs[n_p:]
    g, r2, _, bx, gram = refs[:5]
    uts, pk = refs[5:-1], refs[-1]
    rank, me = pk.shape[0] // 2, lax.axis_index("dp")
    if n_p == 1:
        bx[:2 * rank, :] = split(parts[0][...], 2)
    else:
        rows = parts[0].shape[0]
        for j in range(0, n_p, 2):
            chip = (me ^ j) // 2
            swapped = me % 2 == 1
            first, second = parts[j][...], parts[j + 1][...]
            pair = jnp.concatenate([jnp.where(swapped, second, first), jnp.where(swapped, first, second)], axis=0)
            high = pair.astype(BF16)
            bx[lanes(chip, 2 * rows), :] = high
            bx[pl.ds(pl.multiple_of(rank + chip * 2 * rows, 2 * rows), 2 * rows), :] = (pair - high.astype(F32)).astype(BF16)
    block = pk.shape[1] // ids.shape[1]
    for k in range(ids.shape[1]):
        pk[:, k * block:(k + 1) * block] = bx[:2 * rank, lanes(ids[0, k], block)]
    both = dot(bx[...], bx[:2 * rank, :], NT)
    both = both[:, :rank] + both[:, rank:]
    gram[...] = fold(both[:2 * rank], 2)
    total = fold(dot(split(jnp.transpose(both[2 * rank:]), 3), g[...], NN), 3)
    total = total + fold(dot(pk[...], r2[0], NN), 2) + dot(pk[:rank, :], r2[1], NN)
    if len(uts) == 1:
        uts[0][...] = total
    else:
        half = rank // 2
        low_is_mine = me % 2 == 0
        uts[0][...] = jnp.where(low_is_mine, total[:half], total[half:])
        uts[1][...] = jnp.where(low_is_mine, total[half:], total[:half])


def inverse_factor(gram):
    rank, sub = gram.shape[0], 8
    blocks = rank // sub
    eye = (lax.broadcasted_iota(jnp.int32, (rank, rank), 0) == lax.broadcasted_iota(jnp.int32, (rank, rank), 1)).astype(F32)
    whole = jnp.concatenate([gram, eye], axis=1)
    rows = [whole[b * sub:(b + 1) * sub] for b in range(blocks)]
    place = lax.broadcasted_iota(jnp.int32, (sub, 2 * rank), 0)

    def column(a, k):
        return jnp.take_along_axis(a, jnp.full(a.shape, k, jnp.int32), axis=1)

    out = []
    for b in range(blocks):
        panel = rows[b]
        entry = [column(panel, b * sub + j) for j in range(sub)]
        pivots = jnp.zeros_like(panel)
        scale = []
        for i in range(sub):
            scale.append(1.0 / entry[i][i:i + 1, :])
            pivots = jnp.where(place == i, entry[i], pivots)
            ratio = jnp.where(place > i, entry[i], 0.0) * scale[i]
            panel = panel - ratio * panel[i:i + 1, :]
            for j in range(i + 1, sub):
                entry[j] = entry[j] - ratio * entry[j][i:i + 1, :]
        out.append((panel / jnp.sqrt(pivots))[:, rank:])
        solved = [panel[i:i + 1, :] * scale[i] for i in range(sub)]
        for i in range(sub - 1, -1, -1):
            for j in range(i + 1, sub):
                solved[i] = solved[i] - (entry[j][i:i + 1, :] * scale[i]) * solved[j]
        for c in range(b + 1, blocks):
            update = column(rows[c], b * sub) * solved[0]
            for j in range(1, sub):
                update = update + column(rows[c], b * sub + j) * solved[j]
            rows[c] = rows[c] - update
    return jnp.concatenate(out, axis=0)


def factor_kernel(gram, linv):
    linv[...] = inverse_factor(gram[...])


def left_kernel(ids, linv, bx, pft, blocks):
    rank = linv.shape[0]
    high = linv[...].astype(BF16)
    low = (linv[...] - high.astype(F32)).astype(BF16)
    lhs = jnp.concatenate([high, high, low], axis=1)
    wide = 1024
    for i in range(pft.shape[1] // wide):
        at = slice(i * wide, (i + 1) * wide)
        pft[:, at] = dot(lhs, jnp.concatenate([bx[:2 * rank, at], bx[:rank, at]], axis=0), NN)
    block = blocks.shape[0] // ids.shape[1]
    for k in range(ids.shape[1]):
        piece = jnp.transpose(pft[:, lanes(ids[0, k], block)])
        high = piece.astype(BF16)
        low = (piece - high.astype(F32)).astype(BF16)
        blocks[k * block:(k + 1) * block, :] = jnp.concatenate([high, low, high], axis=1)


def last_kernel(n_u, scale, *refs):
    halves, (linv, blocks, merged, qt, out, ut, right, made, sent) = refs[:n_u], refs[n_u:]
    if n_u == 1:
        ut[...] = halves[0][...]
    else:
        rows, core = halves[0].shape[0], lax.axis_index("dp") % 2
        ut[lanes(core, rows), :] = halves[0][...]
        ut[lanes(1 - core, rows), :] = halves[1][...]
    q = dot(linv[...], ut[...], NN, HIGHEST) * scale
    right[...] = q
    copies = [pltpu.make_async_copy(right, qt, sent.at[merged.shape[0]])]
    copies[0].start()
    two = split(q, 2)
    rank = q.shape[0]
    rhs = jnp.concatenate([two[:rank], two[:rank], two[rank:]], axis=0)
    block = merged.shape[1]
    for k in range(merged.shape[0]):
        made[k] = merged[k] - dot(blocks[k * block:(k + 1) * block, :], rhs, NN)
        copies.append(pltpu.make_async_copy(made.at[k], out.at[k], sent.at[k]))
        copies[-1].start()
    for copy in copies:
        copy.wait()


def gather_rows(x, groups, prepared, first_stage):
    if groups != 4:
        rows = x.shape[0]
        whole = lax.all_gather(x, "mp", axis=0, tiled=True)
        pieces = [whole[j * rows:(j + 1) * rows] for j in range(groups)]
        done = first_stage(pieces[:-2], [(j, None) for j in range(groups - 2)], 0)
        return done, [(pieces[j:j + 1], [(0, None)]) for j in (groups - 2, groups - 1)]
    outer = [(0, 1), (1, 0), (2, 3), (3, 2)]
    inner = [(1, 2), (2, 1)]
    a0 = lax.ppermute(x, "mp", outer)
    b0 = lax.ppermute(together(x, lax.axis_index("mp") * 2)[0], "mp", inner)
    a0, _ = together(a0, prepared)
    b1 = lax.ppermute(a0, "mp", inner)
    a1 = lax.ppermute(b0, "mp", outer)
    done = first_stage([a0], [(0, None)], x.shape[0])
    b1, *done = together(b1, *done)
    cut = x.shape[1] * 3 // 4
    a2 = [lax.ppermute(part, "mp", outer) for part in (b1[:, :cut], b1[:, cut:])]
    return done, [([a1, b0], [(0, 1)]), ([a2[0], b1], [(0, 1)]), ([a2[1], b1], [(0, 1)])]


def swap(a, bit, size):
    return lax.ppermute(a, "dp", [(i, i ^ bit) for i in range(size)])


def together(*values):
    return lax.optimization_barrier(values)


def shards(gen_rows, lengths, assign, rewards, upstream, weight, q_init, resid, block_ids):
    groups, replicas = lax.axis_size("mp"), lax.axis_size("dp")
    slot_count, depth = gen_rows.shape
    columns, rank = q_init.shape
    kept, block = resid.shape[:2]
    rows = groups * slot_count
    ids = block_ids.reshape(1, kept)
    direct = replicas == 8
    shape = jax.ShapeDtypeStruct
    wide_rows, grad_rows = shape((2 * rank + rows, depth), BF16), shape((rows, columns), BF16)

    far = (lengths, assign, rewards, ids, upstream, q_init.T, resid, weight, gen_rows)
    far = [pltpu.with_memory_space_constraint(a, pltpu.HBM) for a in far]
    ids, weight, resid, bx, weighted, q3, r2, pt = call(
        functools.partial(prepare_kernel, replicas if direct else 1, groups == 4),
        [shape(ids.shape, jnp.int32), shape(weight.shape, BF16), shape(resid.shape, F32), wide_rows,
         shape((rows, columns), F32), shape((3 * rank, columns), BF16), shape((2, kept * block, columns), BF16),
         shape((rank, depth), F32)],
        [pltpu.VMEM((rank, columns), F32), pltpu.VMEM(upstream.shape, BF16), pltpu.VMEM((rank, columns), F32),
         pltpu.VMEM(lengths.shape, jnp.int32), pltpu.VMEM(assign.shape, jnp.int32), pltpu.VMEM(rewards.shape, F32),
         pltpu.SemaphoreType.DMA((9,))], name="prepare", far=len(far), grant=PREPARE_GRANT,
    )(*far)

    def stage(pieces, choices, first_row, ready, bx, g, pt, outs, begun=()):
        n = len(pieces)
        cut = depth - pieces[0].shape[1]
        return call(
            functools.partial(next_kernel, n, choices, first_row, ready, cut), [wide_rows, grad_rows] + outs,
            flops=2 * slot_count * depth * columns, name="rows", aliases={n + 4 + len(begun): 0, n + 5 + len(begun): 1},
        )(*pieces, weight, weighted, q3, pt, *begun, bx, g)

    whole_rank = [shape((rank, depth), F32)]
    (bx, g, pt), stages = gather_rows(
        gen_rows, groups, weighted,
        lambda pieces, choices, ready: stage(pieces, choices, 0, ready, bx, jnp.zeros(grad_rows.shape, BF16), pt, whole_rank),
    )
    final = [shape((rank // replicas, depth), F32)] * replicas if direct else whole_rank
    bx, g, pt = stage(*stages[0], rows - 2 * slot_count, 0, bx, g, pt, whole_rank)
    begun = ()
    if len(stages) == 3:
        bx, *begun = call(
            begin_kernel, [wide_rows, shape((slot_count, columns), F32)], name="begin", aliases={3: 0},
        )(weight, *stages[1][0], bx)
    bx, g, *parts = stage(*stages[-1], rows - slot_count, 0, bx, g, pt, final, begun)

    merged = call(merged_kernel, shape((kept, block, columns), F32), name="merged")(ids, bx, g, resid)

    if direct:
        chips = replicas // 2
        sums = [parts[2 * k] + swap(parts[2 * k + 1], 1, replicas) for k in range(chips)]
        got = [swap(sums[k], 2 * k, replicas) for k in range(1, chips)]
        *got, merged = together(*got, merged)
        own = sums[0] + got[0] + got[1] + got[2]
        same = [own] + [swap(own, 2 * k, replicas) for k in range(1, chips)]
        p_parts = []
        for s in same:
            p_parts += [s, swap(s, 1, replicas)]
        u_shapes = [shape((rank // 2, columns), F32)] * 2
    else:
        p_parts = [lax.psum(parts[0], "dp")]
        u_shapes = [shape((rank, columns), F32)]

    n_p = len(p_parts)
    bx, gram, *us = call(
        functools.partial(second_kernel, n_p),
        [wide_rows, shape((rank, rank), F32)] + u_shapes,
        [pltpu.VMEM((2 * rank, kept * block), BF16)], name="second", aliases={n_p + 3: 0},
    )(ids, *p_parts, g, r2, bx)

    linv = call(factor_kernel, shape((rank, rank), F32), name="factor")(gram)

    if direct:
        chip_sum = us[0] + swap(us[1], 1, replicas)
        got = [swap(chip_sum, 2 * k, replicas) for k in range(1, chips)]
        *got, linv = together(*got, linv)
        total = chip_sum + got[0] + got[1] + got[2]
        bx, total = together(bx, total)
        u_parts = [total, swap(total, 1, replicas)]
    else:
        u_parts = [lax.psum(us[0], "dp")]
    pft, blocks = call(
        left_kernel, [shape((rank, depth), F32), shape((kept * block, 3 * rank), BF16)], name="left",
    )(ids, linv, bx)
    if direct:
        other, blocks = together(u_parts[1], blocks)
        u_parts = [u_parts[0], other]
    n_u = len(u_parts)
    qt, new_resid = call(
        functools.partial(last_kernel, n_u, 1.0 / replicas),
        [shape((rank, columns), F32), shape((kept, block, columns), F32)],
        [pltpu.VMEM((rank, columns), F32), pltpu.VMEM((rank, columns), F32),
         pltpu.VMEM((kept, block, columns), F32), pltpu.SemaphoreType.DMA((kept + 1,))],
        name="last", out_specs=[pl.BlockSpec(memory_space=pl.ANY)] * 2,
    )(*u_parts, linv, blocks, merged)
    return pft.T, qt.T, new_resid


def solution(mesh):
    placed = (
        P(("dp", "mp"), None),
        P("dp", None),
        P("dp", None),
        P("dp", None),
        P("dp", "mp"),
        P(None, "mp"),
        P("mp", None),
        P("dp", None, "mp"),
        P("dp"),
    )
    return jax.shard_map(
        shards,
        mesh=mesh,
        in_specs=placed,
        out_specs=(P(None, "mp"), P("mp", None), P("dp", None, "mp")),
        check_vma=False,
    )
```

```python
import functools
import jax
import jax.numpy as jnp
from jax import lax
from jax.experimental import pallas as pl
from jax.experimental.pallas import tpu as pltpu
from jax.sharding import PartitionSpec as P

F32 = jnp.float32
BF16 = jnp.bfloat16
HIGHEST = lax.Precision.HIGHEST
VMEM_LIMIT = 16 * 1024 * 1024
PREPARE_GRANT = 40 * 1024 * 1024


def dot(a, b, dims, precision=None):
    return lax.dot_general(a, b, (dims, ((), ())), precision=precision, preferred_element_type=F32)


NN, NT, TN = ((1,), (0,)), ((1,), (1,)), ((0,), (0,))
VMEM = pl.BlockSpec(memory_space=pltpu.VMEM)
HBM = pl.BlockSpec(memory_space=pltpu.HBM)


def split(a, parts, axis=0):
    out = []
    for _ in range(parts):
        high = a.astype(BF16)
        out.append(high)
        a = a - high.astype(F32)
    return jnp.concatenate(out, axis=axis)


def fold(a, parts):
    rows = a.shape[0] // parts
    total = a[:rows]
    for i in range(1, parts):
        total = total + a[i * rows:(i + 1) * rows]
    return total


def lanes(index, width):
    return pl.ds(pl.multiple_of(index * width, width), width)


def call(kernel, outs, scratch=(), flops=1000000, name=None, aliases=None, out_specs=None, far=0, grant=VMEM_LIMIT):
    def run(*args):
        return pl.pallas_call(
            kernel,
            input_output_aliases=aliases or {},
            out_shape=outs,
            in_specs=[HBM] * far + [VMEM] * (len(args) - far),
            out_specs=out_specs or jax.tree.map(lambda _: VMEM, outs),
            scratch_shapes=list(scratch),
            compiler_params=pltpu.CompilerParams(vmem_limit_bytes=grant),
            cost_estimate=pl.CostEstimate(flops=flops, bytes_accessed=1000000, transcendentals=0),
            name=name,
        )(*args)

    return run


def pick(pieces, choices, out):
    rows = out.shape[0] // len(choices)
    for j, (first, second) in enumerate(choices):
        here = slice(j * rows, (j + 1) * rows)
        if second is None:
            out[here, :] = pieces[first][...]
        else:
            at = lax.axis_index("mp")
            at_end = (at == 0) | (at == lax.axis_size("mp") - 1)

            @pl.when(at_end)
            def _():
                out[here, :] = pieces[first][...]

            @pl.when(jnp.logical_not(at_end))
            def _():
                out[here, :] = pieces[second][...]


def begin_kernel(w, end, between, _, bx, hidden):
    cut = end.shape[1]
    x = bx.at[bx.shape[0] - end.shape[0]:, :cut]
    pick([end, between.at[:, :cut]], [(0, 1)], x)
    hidden[...] = jnp.dot(x[...], w[:cut, :], preferred_element_type=F32)


def weigh_rows(lengths, assign, rewards, upstream, order, weighted):
    groups, sequences = lengths.shape
    slots = upstream.shape[0]
    capacity = slots // (groups * groups)
    count = weighted.shape[0] // groups
    row = lax.broadcasted_iota(jnp.int32, (count, slots), 0)
    slot = lax.broadcasted_iota(jnp.int32, (count, slots), 1)
    row_only = lax.broadcasted_iota(jnp.int32, (count, 1), 0)
    for j, source in enumerate(order):
        picked = jnp.zeros((count, slots), jnp.bool_)
        gain, size = jnp.zeros((count, 1), F32), jnp.ones((count, 1), F32)
        total = rewards[source, 0]
        for s in range(1, sequences):
            total = total + rewards[source, s]
        mean = total * (1.0 / sequences)
        offset = jnp.int32(0)
        for s in range(sequences):
            length = lengths[source, s]
            base = assign[source, s] * (groups * capacity) + source * capacity - offset
            inside = (row >= offset) & (row < offset + length)
            picked = picked | (inside & (slot == row + base))
            inside = (row_only >= offset) & (row_only < offset + length)
            gain = jnp.where(inside, rewards[source, s] - mean, gain)
            size = jnp.where(inside, length.astype(F32), size)
            offset = offset + length
        rows = jnp.dot(picked.astype(F32).astype(BF16), upstream[...], preferred_element_type=F32)
        weighted[j * count:(j + 1) * count, :] = gain / size * rows


def gather_order(groups):
    if groups != 4:
        return list(range(groups))
    at = lax.axis_index("mp")
    low = at < 2
    return [at, at ^ 1, jnp.where(low, 2, 1), jnp.where(low, 3, 0)]


def prepare_kernel(parts, own, *refs):
    small, (upstream_far, q0t_far, resid_far, w, x), refs = refs[:4], refs[4:9], refs[9:]
    ids, w_near, resid, bx, weighted, q3, r2, total, ordered, upstream, q0t, lengths, assign, rewards, arrived = refs
    pairs = list(zip(small, (lengths, assign, rewards, ids)))
    pairs += [(upstream_far, upstream), (q0t_far, q0t), (resid_far, resid), (w, w_near)]
    if own:
        first = bx.shape[0] - weighted.shape[0]
        pairs.append((x, bx.at[first:first + x.shape[0], :]))
    copies = [pltpu.make_async_copy(a, b, arrived.at[i]) for i, (a, b) in enumerate(pairs)]
    for copy in copies:
        copy.start()
    for copy in copies[:5]:
        copy.wait()
    weigh_rows(lengths, assign, rewards, upstream, gather_order(lengths.shape[0]), weighted)
    copies[5].wait()
    rows, me = ordered.shape[0] // parts, lax.axis_index("dp")
    for j in range(parts):
        ordered[j * rows:(j + 1) * rows, :] = q0t[lanes(me ^ j if parts > 1 else 0, rows), :]
    q3[...] = split(ordered[...], 3)
    total[...] = jnp.zeros_like(total)
    copies[6].wait()
    kept, block = resid.shape[:2]
    for k in range(kept):
        total[:, lanes(ids[0, k], block)] += dot(ordered[...], resid[k], NT, HIGHEST)
        high = resid[k].astype(BF16)
        r2[0, k * block:(k + 1) * block, :] = high
        r2[1, k * block:(k + 1) * block, :] = (resid[k] - high.astype(F32)).astype(BF16)
    for copy in copies[7:]:
        copy.wait()


def next_kernel(n_x, choices, first_row, ready, cut, *refs):
    pieces, (w, weighted, q3, before, *refs) = refs[:n_x], refs[n_x:]
    (begun,), refs = (refs[:1], refs[1:]) if cut else ((None,), refs)
    _, _, bx, g, *outs = refs
    count = ready + len(choices) * pieces[0].shape[0]
    top = bx.shape[0] - g.shape[0] + first_row
    x = bx.at[top:top + count, :]
    here = slice(first_row, first_row + count)
    if cut:
        pick([pieces[0], pieces[1].at[:, cut:]], choices, bx.at[top + ready:top + count, cut:])
    else:
        pick(pieces, choices, bx.at[top + ready:top + count, :])
    hidden = jnp.dot(x[:, cut:], w[cut:, :], preferred_element_type=F32)
    if cut:
        hidden = begun[...] + hidden
    tangent = jnp.tanh(hidden)
    grad = (weighted[here, :] * (1.0 - tangent * tangent)).astype(BF16)
    g[here, :] = grad
    yt = split(fold(dot(q3[...], grad, NT), 3), 3, axis=1)
    rows, wide = outs[0].shape[0], 512
    for i in range(bx.shape[1] // wide):
        at = slice(i * wide, (i + 1) * wide)
        total = before[:, at] + dot(yt, jnp.concatenate([x[:, at]] * 3, axis=0), NN)
        for j, out in enumerate(outs):
            out[:, at] = total[j * rows:(j + 1) * rows]


def merged_kernel(ids, bx, g, resid, out):
    block = resid.shape[1]
    for k in range(ids.shape[1]):
        out[k] = dot(bx[bx.shape[0] - g.shape[0]:, lanes(ids[0, k], block)], g[...], TN) + resid[k]


def second_kernel(n_p, ids, *refs):
    parts, refs = refs[:n_p], refs[n_p:]
    g, r2, _, bx, gram = refs[:5]
    uts, pk = refs[5:-1], refs[-1]
    rank, me = pk.shape[0] // 2, lax.axis_index("dp")
    if n_p == 1:
        bx[:2 * rank, :] = split(parts[0][...], 2)
    else:
        rows = parts[0].shape[0]
        for j in range(0, n_p, 2):
            chip = (me ^ j) // 2
            swapped = me % 2 == 1
            first, second = parts[j][...], parts[j + 1][...]
            pair = jnp.concatenate([jnp.where(swapped, second, first), jnp.where(swapped, first, second)], axis=0)
            high = pair.astype(BF16)
            bx[lanes(chip, 2 * rows), :] = high
            bx[pl.ds(pl.multiple_of(rank + chip * 2 * rows, 2 * rows), 2 * rows), :] = (pair - high.astype(F32)).astype(BF16)
    block = pk.shape[1] // ids.shape[1]
    for k in range(ids.shape[1]):
        pk[:, k * block:(k + 1) * block] = bx[:2 * rank, lanes(ids[0, k], block)]
    both = dot(bx[...], bx[:2 * rank, :], NT)
    both = both[:, :rank] + both[:, rank:]
    gram[...] = fold(both[:2 * rank], 2)
    total = fold(dot(split(jnp.transpose(both[2 * rank:]), 3), g[...], NN), 3)
    total = total + fold(dot(pk[...], r2[0], NN), 2) + dot(pk[:rank, :], r2[1], NN)
    if len(uts) == 1:
        uts[0][...] = total
    else:
        half = rank // 2
        low_is_mine = me % 2 == 0
        uts[0][...] = jnp.where(low_is_mine, total[:half], total[half:])
        uts[1][...] = jnp.where(low_is_mine, total[half:], total[:half])


def inverse_factor(gram):
    rank, sub = gram.shape[0], 8
    blocks = rank // sub
    eye = (lax.broadcasted_iota(jnp.int32, (rank, rank), 0) == lax.broadcasted_iota(jnp.int32, (rank, rank), 1)).astype(F32)
    whole = jnp.concatenate([gram, eye], axis=1)
    rows = [whole[b * sub:(b + 1) * sub] for b in range(blocks)]
    place = lax.broadcasted_iota(jnp.int32, (sub, 2 * rank), 0)

    def column(a, k):
        return jnp.take_along_axis(a, jnp.full(a.shape, k, jnp.int32), axis=1)

    out = []
    for b in range(blocks):
        panel = rows[b]
        entry = [column(panel, b * sub + j) for j in range(sub)]
        pivots = jnp.zeros_like(panel)
        scale = []
        for i in range(sub):
            scale.append(1.0 / entry[i][i:i + 1, :])
            pivots = jnp.where(place == i, entry[i], pivots)
            ratio = jnp.where(place > i, entry[i], 0.0) * scale[i]
            panel = panel - ratio * panel[i:i + 1, :]
            for j in range(i + 1, sub):
                entry[j] = entry[j] - ratio * entry[j][i:i + 1, :]
        out.append((panel / jnp.sqrt(pivots))[:, rank:])
        solved = [panel[i:i + 1, :] * scale[i] for i in range(sub)]
        for i in range(sub - 1, -1, -1):
            for j in range(i + 1, sub):
                solved[i] = solved[i] - (entry[j][i:i + 1, :] * scale[i]) * solved[j]
        for c in range(b + 1, blocks):
            update = column(rows[c], b * sub) * solved[0]
            for j in range(1, sub):
                update = update + column(rows[c], b * sub + j) * solved[j]
            rows[c] = rows[c] - update
    return jnp.concatenate(out, axis=0)


def factor_kernel(gram, linv):
    linv[...] = inverse_factor(gram[...])


def left_kernel(ids, linv, bx, pft, blocks):
    rank = linv.shape[0]
    high = linv[...].astype(BF16)
    low = (linv[...] - high.astype(F32)).astype(BF16)
    lhs = jnp.concatenate([high, high, low], axis=1)
    wide = 512
    for i in range(pft.shape[1] // wide):
        at = slice(i * wide, (i + 1) * wide)
        pft[:, at] = dot(lhs, jnp.concatenate([bx[:2 * rank, at], bx[:rank, at]], axis=0), NN)
    block = blocks.shape[0] // ids.shape[1]
    for k in range(ids.shape[1]):
        piece = jnp.transpose(pft[:, lanes(ids[0, k], block)])
        high = piece.astype(BF16)
        low = (piece - high.astype(F32)).astype(BF16)
        blocks[k * block:(k + 1) * block, :] = jnp.concatenate([high, low, high], axis=1)


def last_kernel(n_u, scale, *refs):
    halves, (linv, blocks, merged, qt, out, ut, right, made, sent) = refs[:n_u], refs[n_u:]
    if n_u == 1:
        ut[...] = halves[0][...]
    else:
        rows, core = halves[0].shape[0], lax.axis_index("dp") % 2
        ut[lanes(core, rows), :] = halves[0][...]
        ut[lanes(1 - core, rows), :] = halves[1][...]
    q = dot(linv[...], ut[...], NN, HIGHEST) * scale
    right[...] = q
    copies = [pltpu.make_async_copy(right, qt, sent.at[merged.shape[0]])]
    copies[0].start()
    two = split(q, 2)
    rank = q.shape[0]
    rhs = jnp.concatenate([two[:rank], two[:rank], two[rank:]], axis=0)
    block = merged.shape[1]
    for k in range(merged.shape[0]):
        made[k] = merged[k] - dot(blocks[k * block:(k + 1) * block, :], rhs, NN)
        copies.append(pltpu.make_async_copy(made.at[k], out.at[k], sent.at[k]))
        copies[-1].start()
    for copy in copies:
        copy.wait()


def gather_rows(x, groups, prepared, first_stage):
    if groups != 4:
        rows = x.shape[0]
        whole = lax.all_gather(x, "mp", axis=0, tiled=True)
        pieces = [whole[j * rows:(j + 1) * rows] for j in range(groups)]
        done = first_stage(pieces[:-2], [(j, None) for j in range(groups - 2)], 0)
        return done, [(pieces[j:j + 1], [(0, None)]) for j in (groups - 2, groups - 1)]
    outer = [(0, 1), (1, 0), (2, 3), (3, 2)]
    inner = [(1, 2), (2, 1)]
    a0 = lax.ppermute(x, "mp", outer)
    b0 = lax.ppermute(together(x, lax.axis_index("mp") * 2)[0], "mp", inner)
    a0, _ = together(a0, prepared)
    b1 = lax.ppermute(a0, "mp", inner)
    a1 = lax.ppermute(b0, "mp", outer)
    done = first_stage([a0], [(0, None)], x.shape[0])
    b1, *done = together(b1, *done)
    cut = x.shape[1] * 3 // 4
    a2 = [lax.ppermute(part, "mp", outer) for part in (b1[:, :cut], b1[:, cut:])]
    return done, [([a1, b0], [(0, 1)]), ([a2[0], b1], [(0, 1)]), ([a2[1], b1], [(0, 1)])]


def swap(a, bit, size):
    return lax.ppermute(a, "dp", [(i, i ^ bit) for i in range(size)])


def together(*values):
    return lax.optimization_barrier(values)


def shards(gen_rows, lengths, assign, rewards, upstream, weight, q_init, resid, block_ids):
    groups, replicas = lax.axis_size("mp"), lax.axis_size("dp")
    slot_count, depth = gen_rows.shape
    columns, rank = q_init.shape
    kept, block = resid.shape[:2]
    rows = groups * slot_count
    ids = block_ids.reshape(1, kept)
    direct = replicas == 8
    shape = jax.ShapeDtypeStruct
    wide_rows, grad_rows = shape((2 * rank + rows, depth), BF16), shape((rows, columns), BF16)

    far = (lengths, assign, rewards, ids, upstream, q_init.T, resid, weight, gen_rows)
    far = [pltpu.with_memory_space_constraint(a, pltpu.HBM) for a in far]
    ids, weight, resid, bx, weighted, q3, r2, pt = call(
        functools.partial(prepare_kernel, replicas if direct else 1, groups == 4),
        [shape(ids.shape, jnp.int32), shape(weight.shape, BF16), shape(resid.shape, F32), wide_rows,
         shape((rows, columns), F32), shape((3 * rank, columns), BF16), shape((2, kept * block, columns), BF16),
         shape((rank, depth), F32)],
        [pltpu.VMEM((rank, columns), F32), pltpu.VMEM(upstream.shape, BF16), pltpu.VMEM((rank, columns), F32),
         pltpu.VMEM(lengths.shape, jnp.int32), pltpu.VMEM(assign.shape, jnp.int32), pltpu.VMEM(rewards.shape, F32),
         pltpu.SemaphoreType.DMA((9,))], name="prepare", far=len(far), grant=PREPARE_GRANT,
    )(*far)

    def stage(pieces, choices, first_row, ready, bx, g, pt, outs, begun=()):
        n = len(pieces)
        cut = depth - pieces[0].shape[1]
        return call(
            functools.partial(next_kernel, n, choices, first_row, ready, cut), [wide_rows, grad_rows] + outs,
            flops=2 * slot_count * depth * columns, name="rows", aliases={n + 4 + len(begun): 0, n + 5 + len(begun): 1},
        )(*pieces, weight, weighted, q3, pt, *begun, bx, g)

    whole_rank = [shape((rank, depth), F32)]
    (bx, g, pt), stages = gather_rows(
        gen_rows, groups, weighted,
        lambda pieces, choices, ready: stage(pieces, choices, 0, ready, bx, jnp.zeros(grad_rows.shape, BF16), pt, whole_rank),
    )
    final = [shape((rank // replicas, depth), F32)] * replicas if direct else whole_rank
    bx, g, pt = stage(*stages[0], rows - 2 * slot_count, 0, bx, g, pt, whole_rank)
    begun = ()
    if len(stages) == 3:
        bx, *begun = call(
            begin_kernel, [wide_rows, shape((slot_count, columns), F32)], name="begin", aliases={3: 0},
        )(weight, *stages[1][0], bx)
    bx, g, *parts = stage(*stages[-1], rows - slot_count, 0, bx, g, pt, final, begun)

    merged = call(merged_kernel, shape((kept, block, columns), F32), name="merged")(ids, bx, g, resid)

    if direct:
        chips = replicas // 2
        sums = [parts[2 * k] + swap(parts[2 * k + 1], 1, replicas) for k in range(chips)]
        got = [swap(sums[k], 2 * k, replicas) for k in range(1, chips)]
        *got, merged = together(*got, merged)
        own = sums[0] + got[0] + got[1] + got[2]
        same = [own] + [swap(own, 2 * k, replicas) for k in range(1, chips)]
        p_parts = []
        for s in same:
            p_parts += [s, swap(s, 1, replicas)]
        u_shapes = [shape((rank // 2, columns), F32)] * 2
    else:
        p_parts = [lax.psum(parts[0], "dp")]
        u_shapes = [shape((rank, columns), F32)]

    n_p = len(p_parts)
    bx, gram, *us = call(
        functools.partial(second_kernel, n_p),
        [wide_rows, shape((rank, rank), F32)] + u_shapes,
        [pltpu.VMEM((2 * rank, kept * block), BF16)], name="second", aliases={n_p + 3: 0},
    )(ids, *p_parts, g, r2, bx)

    linv = call(factor_kernel, shape((rank, rank), F32), name="factor")(gram)

    if direct:
        chip_sum = us[0] + swap(us[1], 1, replicas)
        got = [swap(chip_sum, 2 * k, replicas) for k in range(1, chips)]
        *got, linv = together(*got, linv)
        total = chip_sum + got[0] + got[1] + got[2]
        bx, total = together(bx, total)
        u_parts = [total, swap(total, 1, replicas)]
    else:
        u_parts = [lax.psum(us[0], "dp")]
    pft, blocks = call(
        left_kernel, [shape((rank, depth), F32), shape((kept * block, 3 * rank), BF16)], name="left",
    )(ids, linv, bx)
    if direct:
        other, blocks = together(u_parts[1], blocks)
        u_parts = [u_parts[0], other]
    n_u = len(u_parts)
    qt, new_resid = call(
        functools.partial(last_kernel, n_u, 1.0 / replicas),
        [shape((rank, columns), F32), shape((kept, block, columns), F32)],
        [pltpu.VMEM((rank, columns), F32), pltpu.VMEM((rank, columns), F32),
         pltpu.VMEM((kept, block, columns), F32), pltpu.SemaphoreType.DMA((kept + 1,))],
        name="last", out_specs=[pl.BlockSpec(memory_space=pl.ANY)] * 2,
    )(*u_parts, linv, blocks, merged)
    return pft.T, qt.T, new_resid


def solution(mesh):
    placed = (
        P(("dp", "mp"), None),
        P("dp", None),
        P("dp", None),
        P("dp", None),
        P("dp", "mp"),
        P(None, "mp"),
        P("mp", None),
        P("dp", None, "mp"),
        P("dp"),
    )
    return jax.shard_map(
        shards,
        mesh=mesh,
        in_specs=placed,
        out_specs=(P(None, "mp"), P("mp", None), P("dp", None, "mp")),
        check_vma=False,
    )
```

```python
import functools
import jax
import jax.numpy as jnp
from jax import lax
from jax.experimental import pallas as pl
from jax.experimental.pallas import tpu as pltpu
from jax.sharding import PartitionSpec as P

F32 = jnp.float32
BF16 = jnp.bfloat16
HIGHEST = lax.Precision.HIGHEST
VMEM_LIMIT = 16 * 1024 * 1024
LEFT_TILE = 1024
PREPARE_GRANT = 40 * 1024 * 1024


def dot(a, b, dims, precision=None):
    return lax.dot_general(a, b, (dims, ((), ())), precision=precision, preferred_element_type=F32)


NN, NT, TN = ((1,), (0,)), ((1,), (1,)), ((0,), (0,))
VMEM = pl.BlockSpec(memory_space=pltpu.VMEM)
HBM = pl.BlockSpec(memory_space=pltpu.HBM)


def split(a, parts, axis=0):
    out = []
    for _ in range(parts):
        high = a.astype(BF16)
        out.append(high)
        a = a - high.astype(F32)
    return jnp.concatenate(out, axis=axis)


def fold(a, parts):
    rows = a.shape[0] // parts
    total = a[:rows]
    for i in range(1, parts):
        total = total + a[i * rows:(i + 1) * rows]
    return total


def lanes(index, width):
    return pl.ds(pl.multiple_of(index * width, width), width)


def call(kernel, outs, scratch=(), flops=1000000, name=None, aliases=None, out_specs=None, far=0, grant=VMEM_LIMIT):
    def run(*args):
        return pl.pallas_call(
            kernel,
            input_output_aliases=aliases or {},
            out_shape=outs,
            in_specs=[HBM] * far + [VMEM] * (len(args) - far),
            out_specs=out_specs or jax.tree.map(lambda _: VMEM, outs),
            scratch_shapes=list(scratch),
            compiler_params=pltpu.CompilerParams(vmem_limit_bytes=grant),
            cost_estimate=pl.CostEstimate(flops=flops, bytes_accessed=1000000, transcendentals=0),
            name=name,
        )(*args)

    return run


def pick(pieces, choices, out):
    rows = out.shape[0] // len(choices)
    for j, (first, second) in enumerate(choices):
        here = slice(j * rows, (j + 1) * rows)
        if second is None:
            out[here, :] = pieces[first][...]
        else:
            at = lax.axis_index("mp")
            at_end = (at == 0) | (at == lax.axis_size("mp") - 1)

            @pl.when(at_end)
            def _():
                out[here, :] = pieces[first][...]

            @pl.when(jnp.logical_not(at_end))
            def _():
                out[here, :] = pieces[second][...]


def begin_kernel(w, end, between, _, bx, hidden):
    cut = end.shape[1]
    x = bx.at[bx.shape[0] - end.shape[0]:, :cut]
    pick([end, between.at[:, :cut]], [(0, 1)], x)
    hidden[...] = jnp.dot(x[...], w[:cut, :], preferred_element_type=F32)


def weigh_rows(lengths, assign, rewards, upstream, order, weighted):
    groups, sequences = lengths.shape
    slots = upstream.shape[0]
    capacity = slots // (groups * groups)
    count = weighted.shape[0] // groups
    row = lax.broadcasted_iota(jnp.int32, (count, slots), 0)
    slot = lax.broadcasted_iota(jnp.int32, (count, slots), 1)
    row_only = lax.broadcasted_iota(jnp.int32, (count, 1), 0)
    for j, source in enumerate(order):
        picked = jnp.zeros((count, slots), jnp.bool_)
        gain, size = jnp.zeros((count, 1), F32), jnp.ones((count, 1), F32)
        total = rewards[source, 0]
        for s in range(1, sequences):
            total = total + rewards[source, s]
        mean = total * (1.0 / sequences)
        offset = jnp.int32(0)
        for s in range(sequences):
            length = lengths[source, s]
            base = assign[source, s] * (groups * capacity) + source * capacity - offset
            inside = (row >= offset) & (row < offset + length)
            picked = picked | (inside & (slot == row + base))
            inside = (row_only >= offset) & (row_only < offset + length)
            gain = jnp.where(inside, rewards[source, s] - mean, gain)
            size = jnp.where(inside, length.astype(F32), size)
            offset = offset + length
        rows = jnp.dot(picked.astype(F32).astype(BF16), upstream[...], preferred_element_type=F32)
        weighted[j * count:(j + 1) * count, :] = gain / size * rows


def gather_order(groups):
    if groups != 4:
        return list(range(groups))
    at = lax.axis_index("mp")
    low = at < 2
    return [at, at ^ 1, jnp.where(low, 2, 1), jnp.where(low, 3, 0)]


def prepare_kernel(parts, own, *refs):
    small, (upstream_far, q0t_far, resid_far, w, x), refs = refs[:4], refs[4:9], refs[9:]
    ids, w_near, resid, bx, weighted, q3, r2, total, ordered, upstream, q0t, lengths, assign, rewards, arrived = refs
    pairs = list(zip(small, (lengths, assign, rewards, ids)))
    pairs += [(upstream_far, upstream), (q0t_far, q0t), (resid_far, resid), (w, w_near)]
    if own:
        first = bx.shape[0] - weighted.shape[0]
        pairs.append((x, bx.at[first:first + x.shape[0], :]))
    copies = [pltpu.make_async_copy(a, b, arrived.at[i]) for i, (a, b) in enumerate(pairs)]
    for copy in copies:
        copy.start()
    for copy in copies[:5]:
        copy.wait()
    weigh_rows(lengths, assign, rewards, upstream, gather_order(lengths.shape[0]), weighted)
    copies[5].wait()
    rows, me = ordered.shape[0] // parts, lax.axis_index("dp")
    for j in range(parts):
        ordered[j * rows:(j + 1) * rows, :] = q0t[lanes(me ^ j if parts > 1 else 0, rows), :]
    q3[...] = split(ordered[...], 3)
    total[...] = jnp.zeros_like(total)
    copies[6].wait()
    kept, block = resid.shape[:2]
    for k in range(kept):
        total[:, lanes(ids[0, k], block)] += dot(ordered[...], resid[k], NT, HIGHEST)
        high = resid[k].astype(BF16)
        r2[0, k * block:(k + 1) * block, :] = high
        r2[1, k * block:(k + 1) * block, :] = (resid[k] - high.astype(F32)).astype(BF16)
    for copy in copies[7:]:
        copy.wait()


def next_kernel(n_x, choices, first_row, ready, cut, *refs):
    pieces, (w, weighted, q3, before, *refs) = refs[:n_x], refs[n_x:]
    (begun,), refs = (refs[:1], refs[1:]) if cut else ((None,), refs)
    _, _, bx, g, *outs = refs
    count = ready + len(choices) * pieces[0].shape[0]
    top = bx.shape[0] - g.shape[0] + first_row
    x = bx.at[top:top + count, :]
    here = slice(first_row, first_row + count)
    if cut:
        pick([pieces[0], pieces[1].at[:, cut:]], choices, bx.at[top + ready:top + count, cut:])
    else:
        pick(pieces, choices, bx.at[top + ready:top + count, :])
    hidden = jnp.dot(x[:, cut:], w[cut:, :], preferred_element_type=F32)
    if cut:
        hidden = begun[...] + hidden
    tangent = jnp.tanh(hidden)
    grad = (weighted[here, :] * (1.0 - tangent * tangent)).astype(BF16)
    g[here, :] = grad
    yt = split(fold(dot(q3[...], grad, NT), 3), 3, axis=1)
    rows, wide = outs[0].shape[0], 1024
    for i in range(bx.shape[1] // wide):
        at = slice(i * wide, (i + 1) * wide)
        total = before[:, at] + dot(yt, jnp.concatenate([x[:, at]] * 3, axis=0), NN)
        for j, out in enumerate(outs):
            out[:, at] = total[j * rows:(j + 1) * rows]


def merged_kernel(ids, bx, g, resid, out):
    block = resid.shape[1]
    for k in range(ids.shape[1]):
        out[k] = dot(bx[bx.shape[0] - g.shape[0]:, lanes(ids[0, k], block)], g[...], TN) + resid[k]


def second_kernel(n_p, ids, *refs):
    parts, refs = refs[:n_p], refs[n_p:]
    g, r2, _, bx, gram = refs[:5]
    uts, pk = refs[5:-1], refs[-1]
    rank, me = pk.shape[0] // 2, lax.axis_index("dp")
    if n_p == 1:
        bx[:2 * rank, :] = split(parts[0][...], 2)
    else:
        rows = parts[0].shape[0]
        for j in range(0, n_p, 2):
            chip = (me ^ j) // 2
            swapped = me % 2 == 1
            first, second = parts[j][...], parts[j + 1][...]
            pair = jnp.concatenate([jnp.where(swapped, second, first), jnp.where(swapped, first, second)], axis=0)
            high = pair.astype(BF16)
            bx[lanes(chip, 2 * rows), :] = high
            bx[pl.ds(pl.multiple_of(rank + chip * 2 * rows, 2 * rows), 2 * rows), :] = (pair - high.astype(F32)).astype(BF16)
    block = pk.shape[1] // ids.shape[1]
    for k in range(ids.shape[1]):
        pk[:, k * block:(k + 1) * block] = bx[:2 * rank, lanes(ids[0, k], block)]
    both = dot(bx[...], bx[:2 * rank, :], NT)
    both = both[:, :rank] + both[:, rank:]
    gram[...] = fold(both[:2 * rank], 2)
    total = fold(dot(split(jnp.transpose(both[2 * rank:]), 3), g[...], NN), 3)
    total = total + fold(dot(pk[...], r2[0], NN), 2) + dot(pk[:rank, :], r2[1], NN)
    if len(uts) == 1:
        uts[0][...] = total
    else:
        half = rank // 2
        low_is_mine = me % 2 == 0
        uts[0][...] = jnp.where(low_is_mine, total[:half], total[half:])
        uts[1][...] = jnp.where(low_is_mine, total[half:], total[:half])


def inverse_factor(gram):
    rank, sub = gram.shape[0], 8
    blocks = rank // sub
    eye = (lax.broadcasted_iota(jnp.int32, (rank, rank), 0) == lax.broadcasted_iota(jnp.int32, (rank, rank), 1)).astype(F32)
    whole = jnp.concatenate([gram, eye], axis=1)
    rows = [whole[b * sub:(b + 1) * sub] for b in range(blocks)]
    place = lax.broadcasted_iota(jnp.int32, (sub, 2 * rank), 0)

    def column(a, k):
        return jnp.take_along_axis(a, jnp.full(a.shape, k, jnp.int32), axis=1)

    out = []
    for b in range(blocks):
        panel = rows[b]
        entry = [column(panel, b * sub + j) for j in range(sub)]
        pivots = jnp.zeros_like(panel)
        scale = []
        for i in range(sub):
            scale.append(1.0 / entry[i][i:i + 1, :])
            pivots = jnp.where(place == i, entry[i], pivots)
            ratio = jnp.where(place > i, entry[i], 0.0) * scale[i]
            panel = panel - ratio * panel[i:i + 1, :]
            for j in range(i + 1, sub):
                entry[j] = entry[j] - ratio * entry[j][i:i + 1, :]
        out.append((panel / jnp.sqrt(pivots))[:, rank:])
        solved = [panel[i:i + 1, :] * scale[i] for i in range(sub)]
        for i in range(sub - 1, -1, -1):
            for j in range(i + 1, sub):
                solved[i] = solved[i] - (entry[j][i:i + 1, :] * scale[i]) * solved[j]
        for c in range(b + 1, blocks):
            update = column(rows[c], b * sub) * solved[0]
            for j in range(1, sub):
                update = update + column(rows[c], b * sub + j) * solved[j]
            rows[c] = rows[c] - update
    return jnp.concatenate(out, axis=0)


def factor_kernel(gram, linv):
    linv[...] = inverse_factor(gram[...])


def left_kernel(ids, linv, bx, out, blocks, pft, sent):
    rank = linv.shape[0]
    high = linv[...].astype(BF16)
    low = (linv[...] - high.astype(F32)).astype(BF16)
    lhs = jnp.concatenate([high, high, low], axis=1)
    copies, wide = [], LEFT_TILE
    for i in range(pft.shape[1] // wide):
        at = slice(i * wide, (i + 1) * wide)
        pft[:, at] = dot(lhs, jnp.concatenate([bx[:2 * rank, at], bx[:rank, at]], axis=0), NN)
        copies.append(pltpu.make_async_copy(pft.at[:, at], out.at[:, at], sent.at[i]))
        copies[-1].start()
    block = blocks.shape[0] // ids.shape[1]
    for k in range(ids.shape[1]):
        piece = jnp.transpose(pft[:, lanes(ids[0, k], block)])
        high = piece.astype(BF16)
        low = (piece - high.astype(F32)).astype(BF16)
        blocks[k * block:(k + 1) * block, :] = jnp.concatenate([high, low, high], axis=1)
    for copy in copies:
        copy.wait()


def last_kernel(n_u, scale, *refs):
    halves, (linv, blocks, merged, qt, out, ut, right, made, sent) = refs[:n_u], refs[n_u:]
    if n_u == 1:
        ut[...] = halves[0][...]
    else:
        rows, core = halves[0].shape[0], lax.axis_index("dp") % 2
        ut[lanes(core, rows), :] = halves[0][...]
        ut[lanes(1 - core, rows), :] = halves[1][...]
    q = dot(linv[...], ut[...], NN, HIGHEST) * scale
    right[...] = q
    copies = [pltpu.make_async_copy(right, qt, sent.at[merged.shape[0]])]
    copies[0].start()
    two = split(q, 2)
    rank = q.shape[0]
    rhs = jnp.concatenate([two[:rank], two[:rank], two[rank:]], axis=0)
    block = merged.shape[1]
    for k in range(merged.shape[0]):
        made[k] = merged[k] - dot(blocks[k * block:(k + 1) * block, :], rhs, NN)
        copies.append(pltpu.make_async_copy(made.at[k], out.at[k], sent.at[k]))
        copies[-1].start()
    for copy in copies:
        copy.wait()


def gather_rows(x, groups, prepared, first_stage):
    if groups != 4:
        rows = x.shape[0]
        whole = lax.all_gather(x, "mp", axis=0, tiled=True)
        pieces = [whole[j * rows:(j + 1) * rows] for j in range(groups)]
        done = first_stage(pieces[:-2], [(j, None) for j in range(groups - 2)], 0)
        return done, [(pieces[j:j + 1], [(0, None)]) for j in (groups - 2, groups - 1)]
    outer = [(0, 1), (1, 0), (2, 3), (3, 2)]
    inner = [(1, 2), (2, 1)]
    a0 = lax.ppermute(x, "mp", outer)
    b0 = lax.ppermute(together(x, lax.axis_index("mp") * 2)[0], "mp", inner)
    a0, _ = together(a0, prepared)
    b1 = lax.ppermute(a0, "mp", inner)
    a1 = lax.ppermute(b0, "mp", outer)
    done = first_stage([a0], [(0, None)], x.shape[0])
    b1, *done = together(b1, *done)
    cut = x.shape[1] * 3 // 4
    a2 = [lax.ppermute(part, "mp", outer) for part in (b1[:, :cut], b1[:, cut:])]
    return done, [([a1, b0], [(0, 1)]), ([a2[0], b1], [(0, 1)]), ([a2[1], b1], [(0, 1)])]


def swap(a, bit, size):
    return lax.ppermute(a, "dp", [(i, i ^ bit) for i in range(size)])


def together(*values):
    return lax.optimization_barrier(values)


def shards(gen_rows, lengths, assign, rewards, upstream, weight, q_init, resid, block_ids):
    groups, replicas = lax.axis_size("mp"), lax.axis_size("dp")
    slot_count, depth = gen_rows.shape
    columns, rank = q_init.shape
    kept, block = resid.shape[:2]
    rows = groups * slot_count
    ids = block_ids.reshape(1, kept)
    direct = replicas == 8
    shape = jax.ShapeDtypeStruct
    wide_rows, grad_rows = shape((2 * rank + rows, depth), BF16), shape((rows, columns), BF16)

    far = (lengths, assign, rewards, ids, upstream, q_init.T, resid, weight, gen_rows)
    far = [pltpu.with_memory_space_constraint(a, pltpu.HBM) for a in far]
    ids, weight, resid, bx, weighted, q3, r2, pt = call(
        functools.partial(prepare_kernel, replicas if direct else 1, groups == 4),
        [shape(ids.shape, jnp.int32), shape(weight.shape, BF16), shape(resid.shape, F32), wide_rows,
         shape((rows, columns), F32), shape((3 * rank, columns), BF16), shape((2, kept * block, columns), BF16),
         shape((rank, depth), F32)],
        [pltpu.VMEM((rank, columns), F32), pltpu.VMEM(upstream.shape, BF16), pltpu.VMEM((rank, columns), F32),
         pltpu.VMEM(lengths.shape, jnp.int32), pltpu.VMEM(assign.shape, jnp.int32), pltpu.VMEM(rewards.shape, F32),
         pltpu.SemaphoreType.DMA((9,))], name="prepare", far=len(far), grant=PREPARE_GRANT,
    )(*far)

    def stage(pieces, choices, first_row, ready, bx, g, pt, outs, begun=()):
        n = len(pieces)
        cut = depth - pieces[0].shape[1]
        return call(
            functools.partial(next_kernel, n, choices, first_row, ready, cut), [wide_rows, grad_rows] + outs,
            flops=2 * slot_count * depth * columns, name="rows", aliases={n + 4 + len(begun): 0, n + 5 + len(begun): 1},
        )(*pieces, weight, weighted, q3, pt, *begun, bx, g)

    whole_rank = [shape((rank, depth), F32)]
    (bx, g, pt), stages = gather_rows(
        gen_rows, groups, weighted,
        lambda pieces, choices, ready: stage(pieces, choices, 0, ready, bx, jnp.zeros(grad_rows.shape, BF16), pt, whole_rank),
    )
    final = [shape((rank // replicas, depth), F32)] * replicas if direct else whole_rank
    bx, g, pt = stage(*stages[0], rows - 2 * slot_count, 0, bx, g, pt, whole_rank)
    begun = ()
    if len(stages) == 3:
        bx, *begun = call(
            begin_kernel, [wide_rows, shape((slot_count, columns), F32)], name="begin", aliases={3: 0},
        )(weight, *stages[1][0], bx)
    bx, g, *parts = stage(*stages[-1], rows - slot_count, 0, bx, g, pt, final, begun)

    merged = call(merged_kernel, shape((kept, block, columns), F32), name="merged")(ids, bx, g, resid)

    if direct:
        chips = replicas // 2
        sums = [parts[2 * k] + swap(parts[2 * k + 1], 1, replicas) for k in range(chips)]
        got = [swap(sums[k], 2 * k, replicas) for k in range(1, chips)]
        *got, merged = together(*got, merged)
        own = sums[0] + got[0] + got[1] + got[2]
        same = [own] + [swap(own, 2 * k, replicas) for k in range(1, chips)]
        p_parts = []
        for s in same:
            p_parts += [s, swap(s, 1, replicas)]
        u_shapes = [shape((rank // 2, columns), F32)] * 2
    else:
        p_parts = [lax.psum(parts[0], "dp")]
        u_shapes = [shape((rank, columns), F32)]

    n_p = len(p_parts)
    bx, gram, *us = call(
        functools.partial(second_kernel, n_p),
        [wide_rows, shape((rank, rank), F32)] + u_shapes,
        [pltpu.VMEM((2 * rank, kept * block), BF16)], name="second", aliases={n_p + 3: 0},
    )(ids, *p_parts, g, r2, bx)

    linv = call(factor_kernel, shape((rank, rank), F32), name="factor")(gram)

    if direct:
        chip_sum = us[0] + swap(us[1], 1, replicas)
        got = [swap(chip_sum, 2 * k, replicas) for k in range(1, chips)]
        *got, linv = together(*got, linv)
        total = chip_sum + got[0] + got[1] + got[2]
        bx, total = together(bx, total)
        u_parts = [total, swap(total, 1, replicas)]
    else:
        u_parts = [lax.psum(us[0], "dp")]
    pft, blocks = call(
        left_kernel, [shape((rank, depth), F32), shape((kept * block, 3 * rank), BF16)],
        [pltpu.VMEM((rank, depth), F32), pltpu.SemaphoreType.DMA((depth // LEFT_TILE,))], name="left",
        out_specs=[pl.BlockSpec(memory_space=pl.ANY), VMEM],
    )(ids, linv, bx)
    if direct:
        other, blocks = together(u_parts[1], blocks)
        u_parts = [u_parts[0], other]
    n_u = len(u_parts)
    qt, new_resid = call(
        functools.partial(last_kernel, n_u, 1.0 / replicas),
        [shape((rank, columns), F32), shape((kept, block, columns), F32)],
        [pltpu.VMEM((rank, columns), F32), pltpu.VMEM((rank, columns), F32),
         pltpu.VMEM((kept, block, columns), F32), pltpu.SemaphoreType.DMA((kept + 1,))],
        name="last", out_specs=[pl.BlockSpec(memory_space=pl.ANY)] * 2,
    )(*u_parts, linv, blocks, merged)
    return pft.T, qt.T, new_resid


def solution(mesh):
    placed = (
        P(("dp", "mp"), None),
        P("dp", None),
        P("dp", None),
        P("dp", None),
        P("dp", "mp"),
        P(None, "mp"),
        P("mp", None),
        P("dp", None, "mp"),
        P("dp"),
    )
    return jax.shard_map(
        shards,
        mesh=mesh,
        in_specs=placed,
        out_specs=(P(None, "mp"), P("mp", None), P("dp", None, "mp")),
        check_vma=False,
    )
```

```python
import functools
import jax
import jax.numpy as jnp
from jax import lax
from jax.experimental import pallas as pl
from jax.experimental.pallas import tpu as pltpu
from jax.sharding import PartitionSpec as P

F32 = jnp.float32
BF16 = jnp.bfloat16
HIGHEST = lax.Precision.HIGHEST
VMEM_LIMIT = 16 * 1024 * 1024
LEFT_TILE = 512
PREPARE_GRANT = 40 * 1024 * 1024


def dot(a, b, dims, precision=None):
    return lax.dot_general(a, b, (dims, ((), ())), precision=precision, preferred_element_type=F32)


NN, NT, TN = ((1,), (0,)), ((1,), (1,)), ((0,), (0,))
VMEM = pl.BlockSpec(memory_space=pltpu.VMEM)
HBM = pl.BlockSpec(memory_space=pltpu.HBM)


def split(a, parts, axis=0):
    out = []
    for _ in range(parts):
        high = a.astype(BF16)
        out.append(high)
        a = a - high.astype(F32)
    return jnp.concatenate(out, axis=axis)


def fold(a, parts):
    rows = a.shape[0] // parts
    total = a[:rows]
    for i in range(1, parts):
        total = total + a[i * rows:(i + 1) * rows]
    return total


def lanes(index, width):
    return pl.ds(pl.multiple_of(index * width, width), width)


def call(kernel, outs, scratch=(), flops=1000000, name=None, aliases=None, out_specs=None, far=0, grant=VMEM_LIMIT):
    def run(*args):
        return pl.pallas_call(
            kernel,
            input_output_aliases=aliases or {},
            out_shape=outs,
            in_specs=[HBM] * far + [VMEM] * (len(args) - far),
            out_specs=out_specs or jax.tree.map(lambda _: VMEM, outs),
            scratch_shapes=list(scratch),
            compiler_params=pltpu.CompilerParams(vmem_limit_bytes=grant),
            cost_estimate=pl.CostEstimate(flops=flops, bytes_accessed=1000000, transcendentals=0),
            name=name,
        )(*args)

    return run


def pick(pieces, choices, out):
    rows = out.shape[0] // len(choices)
    for j, (first, second) in enumerate(choices):
        here = slice(j * rows, (j + 1) * rows)
        if second is None:
            out[here, :] = pieces[first][...]
        else:
            at = lax.axis_index("mp")
            at_end = (at == 0) | (at == lax.axis_size("mp") - 1)

            @pl.when(at_end)
            def _():
                out[here, :] = pieces[first][...]

            @pl.when(jnp.logical_not(at_end))
            def _():
                out[here, :] = pieces[second][...]


def begin_kernel(w, end, between, _, bx, hidden):
    cut = end.shape[1]
    x = bx.at[bx.shape[0] - end.shape[0]:, :cut]
    pick([end, between.at[:, :cut]], [(0, 1)], x)
    hidden[...] = jnp.dot(x[...], w[:cut, :], preferred_element_type=F32)


def weigh_rows(lengths, assign, rewards, upstream, order, weighted):
    groups, sequences = lengths.shape
    slots = upstream.shape[0]
    capacity = slots // (groups * groups)
    count = weighted.shape[0] // groups
    row = lax.broadcasted_iota(jnp.int32, (count, slots), 0)
    slot = lax.broadcasted_iota(jnp.int32, (count, slots), 1)
    row_only = lax.broadcasted_iota(jnp.int32, (count, 1), 0)
    for j, source in enumerate(order):
        picked = jnp.zeros((count, slots), jnp.bool_)
        gain, size = jnp.zeros((count, 1), F32), jnp.ones((count, 1), F32)
        total = rewards[source, 0]
        for s in range(1, sequences):
            total = total + rewards[source, s]
        mean = total * (1.0 / sequences)
        offset = jnp.int32(0)
        for s in range(sequences):
            length = lengths[source, s]
            base = assign[source, s] * (groups * capacity) + source * capacity - offset
            inside = (row >= offset) & (row < offset + length)
            picked = picked | (inside & (slot == row + base))
            inside = (row_only >= offset) & (row_only < offset + length)
            gain = jnp.where(inside, rewards[source, s] - mean, gain)
            size = jnp.where(inside, length.astype(F32), size)
            offset = offset + length
        rows = jnp.dot(picked.astype(F32).astype(BF16), upstream[...], preferred_element_type=F32)
        weighted[j * count:(j + 1) * count, :] = gain / size * rows


def gather_order(groups):
    if groups != 4:
        return list(range(groups))
    at = lax.axis_index("mp")
    low = at < 2
    return [at, at ^ 1, jnp.where(low, 2, 1), jnp.where(low, 3, 0)]


def prepare_kernel(parts, own, *refs):
    small, (upstream_far, q0t_far, resid_far, w, x), refs = refs[:4], refs[4:9], refs[9:]
    ids, w_near, resid, bx, weighted, q3, r2, total, ordered, upstream, q0t, lengths, assign, rewards, arrived = refs
    pairs = list(zip(small, (lengths, assign, rewards, ids)))
    pairs += [(upstream_far, upstream), (q0t_far, q0t), (resid_far, resid), (w, w_near)]
    if own:
        first = bx.shape[0] - weighted.shape[0]
        pairs.append((x, bx.at[first:first + x.shape[0], :]))
    copies = [pltpu.make_async_copy(a, b, arrived.at[i]) for i, (a, b) in enumerate(pairs)]
    for copy in copies:
        copy.start()
    for copy in copies[:5]:
        copy.wait()
    weigh_rows(lengths, assign, rewards, upstream, gather_order(lengths.shape[0]), weighted)
    copies[5].wait()
    rows, me = ordered.shape[0] // parts, lax.axis_index("dp")
    for j in range(parts):
        ordered[j * rows:(j + 1) * rows, :] = q0t[lanes(me ^ j if parts > 1 else 0, rows), :]
    q3[...] = split(ordered[...], 3)
    total[...] = jnp.zeros_like(total)
    copies[6].wait()
    kept, block = resid.shape[:2]
    for k in range(kept):
        total[:, lanes(ids[0, k], block)] += dot(ordered[...], resid[k], NT, HIGHEST)
        high = resid[k].astype(BF16)
        r2[0, k * block:(k + 1) * block, :] = high
        r2[1, k * block:(k + 1) * block, :] = (resid[k] - high.astype(F32)).astype(BF16)
    for copy in copies[7:]:
        copy.wait()


def next_kernel(n_x, choices, first_row, ready, cut, *refs):
    pieces, (w, weighted, q3, before, *refs) = refs[:n_x], refs[n_x:]
    (begun,), refs = (refs[:1], refs[1:]) if cut else ((None,), refs)
    _, _, bx, g, *outs = refs
    count = ready + len(choices) * pieces[0].shape[0]
    top = bx.shape[0] - g.shape[0] + first_row
    x = bx.at[top:top + count, :]
    here = slice(first_row, first_row + count)
    if cut:
        pick([pieces[0], pieces[1].at[:, cut:]], choices, bx.at[top + ready:top + count, cut:])
    else:
        pick(pieces, choices, bx.at[top + ready:top + count, :])
    hidden = jnp.dot(x[:, cut:], w[cut:, :], preferred_element_type=F32)
    if cut:
        hidden = begun[...] + hidden
    tangent = jnp.tanh(hidden)
    grad = (weighted[here, :] * (1.0 - tangent * tangent)).astype(BF16)
    g[here, :] = grad
    yt = split(fold(dot(q3[...], grad, NT), 3), 3, axis=1)
    rows, wide = outs[0].shape[0], 1024
    for i in range(bx.shape[1] // wide):
        at = slice(i * wide, (i + 1) * wide)
        total = before[:, at] + dot(yt, jnp.concatenate([x[:, at]] * 3, axis=0), NN)
        for j, out in enumerate(outs):
            out[:, at] = total[j * rows:(j + 1) * rows]


def merged_kernel(ids, bx, g, resid, out):
    block = resid.shape[1]
    for k in range(ids.shape[1]):
        out[k] = dot(bx[bx.shape[0] - g.shape[0]:, lanes(ids[0, k], block)], g[...], TN) + resid[k]


def second_kernel(n_p, ids, *refs):
    parts, refs = refs[:n_p], refs[n_p:]
    g, r2, _, bx, gram = refs[:5]
    uts, pk = refs[5:-1], refs[-1]
    rank, me = pk.shape[0] // 2, lax.axis_index("dp")
    if n_p == 1:
        bx[:2 * rank, :] = split(parts[0][...], 2)
    else:
        rows = parts[0].shape[0]
        for j in range(0, n_p, 2):
            chip = (me ^ j) // 2
            swapped = me % 2 == 1
            first, second = parts[j][...], parts[j + 1][...]
            pair = jnp.concatenate([jnp.where(swapped, second, first), jnp.where(swapped, first, second)], axis=0)
            high = pair.astype(BF16)
            bx[lanes(chip, 2 * rows), :] = high
            bx[pl.ds(pl.multiple_of(rank + chip * 2 * rows, 2 * rows), 2 * rows), :] = (pair - high.astype(F32)).astype(BF16)
    block = pk.shape[1] // ids.shape[1]
    for k in range(ids.shape[1]):
        pk[:, k * block:(k + 1) * block] = bx[:2 * rank, lanes(ids[0, k], block)]
    both = dot(bx[...], bx[:2 * rank, :], NT)
    both = both[:, :rank] + both[:, rank:]
    gram[...] = fold(both[:2 * rank], 2)
    total = fold(dot(split(jnp.transpose(both[2 * rank:]), 3), g[...], NN), 3)
    total = total + fold(dot(pk[...], r2[0], NN), 2) + dot(pk[:rank, :], r2[1], NN)
    if len(uts) == 1:
        uts[0][...] = total
    else:
        half = rank // 2
        low_is_mine = me % 2 == 0
        uts[0][...] = jnp.where(low_is_mine, total[:half], total[half:])
        uts[1][...] = jnp.where(low_is_mine, total[half:], total[:half])


def inverse_factor(gram):
    rank, sub = gram.shape[0], 8
    blocks = rank // sub
    eye = (lax.broadcasted_iota(jnp.int32, (rank, rank), 0) == lax.broadcasted_iota(jnp.int32, (rank, rank), 1)).astype(F32)
    whole = jnp.concatenate([gram, eye], axis=1)
    rows = [whole[b * sub:(b + 1) * sub] for b in range(blocks)]
    place = lax.broadcasted_iota(jnp.int32, (sub, 2 * rank), 0)

    def column(a, k):
        return jnp.take_along_axis(a, jnp.full(a.shape, k, jnp.int32), axis=1)

    out = []
    for b in range(blocks):
        panel = rows[b]
        entry = [column(panel, b * sub + j) for j in range(sub)]
        pivots = jnp.zeros_like(panel)
        scale = []
        for i in range(sub):
            scale.append(1.0 / entry[i][i:i + 1, :])
            pivots = jnp.where(place == i, entry[i], pivots)
            ratio = jnp.where(place > i, entry[i], 0.0) * scale[i]
            panel = panel - ratio * panel[i:i + 1, :]
            for j in range(i + 1, sub):
                entry[j] = entry[j] - ratio * entry[j][i:i + 1, :]
        out.append((panel / jnp.sqrt(pivots))[:, rank:])
        solved = [panel[i:i + 1, :] * scale[i] for i in range(sub)]
        for i in range(sub - 1, -1, -1):
            for j in range(i + 1, sub):
                solved[i] = solved[i] - (entry[j][i:i + 1, :] * scale[i]) * solved[j]
        for c in range(b + 1, blocks):
            update = column(rows[c], b * sub) * solved[0]
            for j in range(1, sub):
                update = update + column(rows[c], b * sub + j) * solved[j]
            rows[c] = rows[c] - update
    return jnp.concatenate(out, axis=0)


def factor_kernel(gram, linv):
    linv[...] = inverse_factor(gram[...])


def left_kernel(ids, linv, bx, out, blocks, pft, sent):
    rank = linv.shape[0]
    high = linv[...].astype(BF16)
    low = (linv[...] - high.astype(F32)).astype(BF16)
    lhs = jnp.concatenate([high, high, low], axis=1)
    copies, wide = [], LEFT_TILE
    for i in range(pft.shape[1] // wide):
        at = slice(i * wide, (i + 1) * wide)
        pft[:, at] = dot(lhs, jnp.concatenate([bx[:2 * rank, at], bx[:rank, at]], axis=0), NN)
        copies.append(pltpu.make_async_copy(pft.at[:, at], out.at[:, at], sent.at[i]))
        copies[-1].start()
    block = blocks.shape[0] // ids.shape[1]
    for k in range(ids.shape[1]):
        piece = jnp.transpose(pft[:, lanes(ids[0, k], block)])
        high = piece.astype(BF16)
        low = (piece - high.astype(F32)).astype(BF16)
        blocks[k * block:(k + 1) * block, :] = jnp.concatenate([high, low, high], axis=1)
    for copy in copies:
        copy.wait()


def last_kernel(n_u, scale, *refs):
    halves, (linv, blocks, merged, qt, out, ut, right, made, sent) = refs[:n_u], refs[n_u:]
    if n_u == 1:
        ut[...] = halves[0][...]
    else:
        rows, core = halves[0].shape[0], lax.axis_index("dp") % 2
        ut[lanes(core, rows), :] = halves[0][...]
        ut[lanes(1 - core, rows), :] = halves[1][...]
    q = dot(linv[...], ut[...], NN, HIGHEST) * scale
    right[...] = q
    copies = [pltpu.make_async_copy(right, qt, sent.at[merged.shape[0]])]
    copies[0].start()
    two = split(q, 2)
    rank = q.shape[0]
    rhs = jnp.concatenate([two[:rank], two[:rank], two[rank:]], axis=0)
    block = merged.shape[1]
    for k in range(merged.shape[0]):
        made[k] = merged[k] - dot(blocks[k * block:(k + 1) * block, :], rhs, NN)
        copies.append(pltpu.make_async_copy(made.at[k], out.at[k], sent.at[k]))
        copies[-1].start()
    for copy in copies:
        copy.wait()


def gather_rows(x, groups, prepared, first_stage):
    if groups != 4:
        rows = x.shape[0]
        whole = lax.all_gather(x, "mp", axis=0, tiled=True)
        pieces = [whole[j * rows:(j + 1) * rows] for j in range(groups)]
        done = first_stage(pieces[:-2], [(j, None) for j in range(groups - 2)], 0)
        return done, [(pieces[j:j + 1], [(0, None)]) for j in (groups - 2, groups - 1)]
    outer = [(0, 1), (1, 0), (2, 3), (3, 2)]
    inner = [(1, 2), (2, 1)]
    a0 = lax.ppermute(x, "mp", outer)
    b0 = lax.ppermute(together(x, lax.axis_index("mp") * 2)[0], "mp", inner)
    a0, _ = together(a0, prepared)
    b1 = lax.ppermute(a0, "mp", inner)
    a1 = lax.ppermute(b0, "mp", outer)
    done = first_stage([a0], [(0, None)], x.shape[0])
    b1, *done = together(b1, *done)
    cut = x.shape[1] * 3 // 4
    a2 = [lax.ppermute(part, "mp", outer) for part in (b1[:, :cut], b1[:, cut:])]
    return done, [([a1, b0], [(0, 1)]), ([a2[0], b1], [(0, 1)]), ([a2[1], b1], [(0, 1)])]


def swap(a, bit, size):
    return lax.ppermute(a, "dp", [(i, i ^ bit) for i in range(size)])


def together(*values):
    return lax.optimization_barrier(values)


def shards(gen_rows, lengths, assign, rewards, upstream, weight, q_init, resid, block_ids):
    groups, replicas = lax.axis_size("mp"), lax.axis_size("dp")
    slot_count, depth = gen_rows.shape
    columns, rank = q_init.shape
    kept, block = resid.shape[:2]
    rows = groups * slot_count
    ids = block_ids.reshape(1, kept)
    direct = replicas == 8
    shape = jax.ShapeDtypeStruct
    wide_rows, grad_rows = shape((2 * rank + rows, depth), BF16), shape((rows, columns), BF16)

    far = (lengths, assign, rewards, ids, upstream, q_init.T, resid, weight, gen_rows)
    far = [pltpu.with_memory_space_constraint(a, pltpu.HBM) for a in far]
    ids, weight, resid, bx, weighted, q3, r2, pt = call(
        functools.partial(prepare_kernel, replicas if direct else 1, groups == 4),
        [shape(ids.shape, jnp.int32), shape(weight.shape, BF16), shape(resid.shape, F32), wide_rows,
         shape((rows, columns), F32), shape((3 * rank, columns), BF16), shape((2, kept * block, columns), BF16),
         shape((rank, depth), F32)],
        [pltpu.VMEM((rank, columns), F32), pltpu.VMEM(upstream.shape, BF16), pltpu.VMEM((rank, columns), F32),
         pltpu.VMEM(lengths.shape, jnp.int32), pltpu.VMEM(assign.shape, jnp.int32), pltpu.VMEM(rewards.shape, F32),
         pltpu.SemaphoreType.DMA((9,))], name="prepare", far=len(far), grant=PREPARE_GRANT,
    )(*far)

    def stage(pieces, choices, first_row, ready, bx, g, pt, outs, begun=()):
        n = len(pieces)
        cut = depth - pieces[0].shape[1]
        return call(
            functools.partial(next_kernel, n, choices, first_row, ready, cut), [wide_rows, grad_rows] + outs,
            flops=2 * slot_count * depth * columns, name="rows", aliases={n + 4 + len(begun): 0, n + 5 + len(begun): 1},
        )(*pieces, weight, weighted, q3, pt, *begun, bx, g)

    whole_rank = [shape((rank, depth), F32)]
    (bx, g, pt), stages = gather_rows(
        gen_rows, groups, weighted,
        lambda pieces, choices, ready: stage(pieces, choices, 0, ready, bx, jnp.zeros(grad_rows.shape, BF16), pt, whole_rank),
    )
    final = [shape((rank // replicas, depth), F32)] * replicas if direct else whole_rank
    bx, g, pt = stage(*stages[0], rows - 2 * slot_count, 0, bx, g, pt, whole_rank)
    begun = ()
    if len(stages) == 3:
        bx, *begun = call(
            begin_kernel, [wide_rows, shape((slot_count, columns), F32)], name="begin", aliases={3: 0},
        )(weight, *stages[1][0], bx)
    bx, g, *parts = stage(*stages[-1], rows - slot_count, 0, bx, g, pt, final, begun)

    merged = call(merged_kernel, shape((kept, block, columns), F32), name="merged")(ids, bx, g, resid)

    if direct:
        chips = replicas // 2
        sums = [parts[2 * k] + swap(parts[2 * k + 1], 1, replicas) for k in range(chips)]
        got = [swap(sums[k], 2 * k, replicas) for k in range(1, chips)]
        *got, merged = together(*got, merged)
        own = sums[0] + got[0] + got[1] + got[2]
        same = [own] + [swap(own, 2 * k, replicas) for k in range(1, chips)]
        p_parts = []
        for s in same:
            p_parts += [s, swap(s, 1, replicas)]
        u_shapes = [shape((rank // 2, columns), F32)] * 2
    else:
        p_parts = [lax.psum(parts[0], "dp")]
        u_shapes = [shape((rank, columns), F32)]

    n_p = len(p_parts)
    bx, gram, *us = call(
        functools.partial(second_kernel, n_p),
        [wide_rows, shape((rank, rank), F32)] + u_shapes,
        [pltpu.VMEM((2 * rank, kept * block), BF16)], name="second", aliases={n_p + 3: 0},
    )(ids, *p_parts, g, r2, bx)

    linv = call(factor_kernel, shape((rank, rank), F32), name="factor")(gram)

    if direct:
        chip_sum = us[0] + swap(us[1], 1, replicas)
        got = [swap(chip_sum, 2 * k, replicas) for k in range(1, chips)]
        *got, linv = together(*got, linv)
        total = chip_sum + got[0] + got[1] + got[2]
        bx, total = together(bx, total)
        u_parts = [total, swap(total, 1, replicas)]
    else:
        u_parts = [lax.psum(us[0], "dp")]
    pft, blocks = call(
        left_kernel, [shape((rank, depth), F32), shape((kept * block, 3 * rank), BF16)],
        [pltpu.VMEM((rank, depth), F32), pltpu.SemaphoreType.DMA((depth // LEFT_TILE,))], name="left",
        out_specs=[pl.BlockSpec(memory_space=pl.ANY), VMEM],
    )(ids, linv, bx)
    if direct:
        other, blocks = together(u_parts[1], blocks)
        u_parts = [u_parts[0], other]
    n_u = len(u_parts)
    qt, new_resid = call(
        functools.partial(last_kernel, n_u, 1.0 / replicas),
        [shape((rank, columns), F32), shape((kept, block, columns), F32)],
        [pltpu.VMEM((rank, columns), F32), pltpu.VMEM((rank, columns), F32),
         pltpu.VMEM((kept, block, columns), F32), pltpu.SemaphoreType.DMA((kept + 1,))],
        name="last", out_specs=[pl.BlockSpec(memory_space=pl.ANY)] * 2,
    )(*u_parts, linv, blocks, merged)
    return pft.T, qt.T, new_resid


def solution(mesh):
    placed = (
        P(("dp", "mp"), None),
        P("dp", None),
        P("dp", None),
        P("dp", None),
        P("dp", "mp"),
        P(None, "mp"),
        P("mp", None),
        P("dp", None, "mp"),
        P("dp"),
    )
    return jax.shard_map(
        shards,
        mesh=mesh,
        in_specs=placed,
        out_specs=(P(None, "mp"), P("mp", None), P("dp", None, "mp")),
        check_vma=False,
    )
```
